256 devices in a mesh: seq: 16 (over x, y), expert: 16 (over z, core).
Axes of the slice: x: 4, y: 4, z: 8, core: 2. Of those that a mesh axis runs over, the one named last changes fastest.
Arguments:
- tokens: bfloat16 [2048, 4096], P('seq'), may hold values from -8 to 8
- norm_gain: float32 [4096], replicated, may hold values from 0.25 to 1.75
- in_weight: bfloat16 [4096, 2, 8192], P('seq', None, 'expert'), may hold values from -0.09375 to 0.09375
- conv_weight: float32 [4, 8192], P(None, 'expert'), may hold values from -0.5 to 0.5
- conv_bias: float32 [8192], P('expert'), may hold values from -0.5 to 0.5
- proj_weight: bfloat16 [8192, 288], P('expert'), may hold values from -0.0625 to 0.0625
- step_weight: bfloat16 [256, 8192], P(None, 'expert'), may hold values from -1 to 1
- step_bias: float32 [8192], P('expert'), may hold values from -5 to -1
- decay_log: float32 [8192, 16], P('expert'), may hold values from -6 to 2.7
- skip_gain: float32 [8192], P('expert'), may hold values from 0.5 to 1.5
- out_weight: bfloat16 [8192, 4096], P('expert', 'seq'), may hold values from -0.0625 to 0.0625
- moe_gain: float32 [4096], replicated, may hold values from 0.25 to 1.75
- router_weight: bfloat16 [4096, 16], replicated, may hold values from -0.09375 to 0.09375
- routes: int32 [2048, 2], P(('seq', 'expert')), may hold values from 0 to 15, all different within a row; in each aligned block of 8 rows (0 to 7, 8 to 15, ...) at most 2 rows name the same one
- gate_weight: bfloat16 [16, 4096, 7168], P('expert', None, 'seq'), may hold values from -0.09375 to 0.09375
- up_weight: bfloat16 [16, 4096, 7168], P('expert', None, 'seq'), may hold values from -0.09375 to 0.09375
- down_weight: bfloat16 [16, 7168, 4096], P('expert', 'seq'), may hold values from -0.0625 to 0.0625
Outputs:
- mixed: bfloat16 [2048, 4096], P(('seq', 'expert'))
The draws below stay inside these ranges and needn't reach their ends.
Inputs may be any that keep to these rules, and one draw needn't show every extreme that they name: `routes`: each row names two different experts; within each aligned block of 8 rows no expert is named by more than 2 rows, and that number is reached in some blocks.
All inputs are finite; a program needn't handle non-finite values.
Results may differ from the reference program's by a relative error of at most 0.013.
Values may be sent and summed in bfloat16 or wider, within the bound.
A program may use at most 128 MiB of HBM per device.

```python
import math
import jax
import jax.numpy as jnp
import numpy as np
from jax import lax

D = 4096
DI = 8192
STATE = 16
RANK = 256
CONV = 4
FF = 7168
TOK_SEQ = 128
TOKENS = 2048
EXPERTS = 16
BLOCK = 8
MOST = 2
N_SEQ = 16


def draw_tokens(key, part):
    noise_key, shard_key = jax.random.split(jax.random.fold_in(key, 17))
    noise = jax.random.normal(noise_key, (TOKENS, D), jnp.float32)
    lift = 1.5
    shard_rows = jax.random.normal(shard_key, (TOKENS // TOK_SEQ, D), jnp.float32)
    common = jnp.repeat(shard_rows, TOK_SEQ, axis=0)
    return jnp.clip(noise + lift * common, -8.0, 8.0).astype(jnp.bfloat16)


def block_scale(stream_key, dims, shards, least, top_value):
    def one(dim, parts):
        heights = jax.random.uniform(jax.random.fold_in(jax.random.fold_in(stream_key, 6), dim), (parts,), jnp.float32, least / len(shards), top_value / len(shards))
        return jnp.repeat(jnp.exp(heights), dims[dim] // parts).reshape((-1,) + (1,) * (len(dims) - dim - 1))

    factor_of = one(*shards[0])
    for cut in shards[1:]:
        factor_of = factor_of * one(*cut)
    return factor_of


def shared_out(own_key, own, number, rows, count, top, limit, slope):
    order = jax.random.permutation(own_key, count)
    heavy_load, usual = load_shares(count, rows * top, limit, slope, True), load_shares(count, rows * top, limit, slope, False)
    places = jnp.arange(count)

    def named(tallies, rotation):
        used = int((tallies > 0).sum())
        fixed = max(1, used // 4)
        moved = fixed + (places - fixed + rotation * (used - fixed)) % max(1, count - fixed)
        return jnp.zeros((count,), jnp.int32).at[order[jnp.where(places < fixed, places, moved)]].set(jnp.asarray(tallies, jnp.int32))

    tallies = jnp.where(number % 4 == 0, named(heavy_load, number // 4), named(usual, number - number // 4 - 1))
    mixed = jax.random.permutation(jax.random.fold_in(own, 3), count)
    source_of, sink = mixed[0:count // 2 * 2:2], mixed[1:count // 2 * 2:2]
    room = jnp.minimum(tallies[source_of] - 1, limit - tallies[sink]) // 2
    room = jnp.where((source_of == order[0]) | (sink == order[0]) | (tallies[sink] == 0), 0, jnp.maximum(room, 0))
    moved = jax.random.randint(jax.random.fold_in(own, 4), (count // 2,), 0, 1 << 20) % (room + 1)
    tallies = tallies.at[source_of].add(-moved).at[sink].add(moved)
    members = jnp.searchsorted(jnp.cumsum(tallies), jnp.arange(rows * top), side="right").astype(jnp.int32)
    listing = members.reshape(top, rows).T
    listing = listing[jax.random.permutation(jax.random.fold_in(own, 1), rows)]
    rotation = jax.random.randint(jax.random.fold_in(own, 2), (rows, 1), 0, top)
    return jnp.take_along_axis(listing, (jnp.arange(top)[None, :] + rotation) % top, axis=1)


def load_shares(count, total, most, slope, full):
    loads = [(1 << 20) // math.isqrt(standing ** slope) + 1 for standing in range(1, count + 1)]
    largest = most if full else min(most, max(-(-total // count), total * loads[0] // sum(loads)))
    least = 1 if total - largest >= count - 1 else 0
    given, rest = [largest] + [least] * (count - 1), total - largest - least * (count - 1)
    while rest > 0:
        candidates = [i for i in range(1, count) if given[i] < largest] or [i for i in range(1, count) if given[i] < most]
        pool, remaining = sum([loads[i] for i in candidates]), rest
        for i in candidates:
            addition = min(most - given[i], max(1, remaining * loads[i] // pool), rest)
            given[i] = given[i] + addition
            rest = rest - addition
    return np.array(given)


def centred(rng, dims, width, limit, shards=(), held_as=jnp.bfloat16):
    factor_of = block_scale(rng, dims, shards, -0.22, 0.18) if shards else 1.0
    values = jax.random.normal(rng, dims, jnp.float32) * width * factor_of
    return jnp.minimum(jnp.maximum(values, -limit), limit).astype(held_as)


def setup_inputs(seed: int = 0) -> dict:
    key_of = jax.random.split(jax.random.key(seed), 18)
    tokens = draw_tokens(jax.random.fold_in(key_of[17], 71), 0)
    norm_gain = jnp.clip(1.0 + 0.15 * jax.random.normal(key_of[1], (D,), jnp.float32), 0.25, 1.75)
    in_weight = centred(key_of[2], (D, 2, DI), D ** -0.5, 0.09375, ((0, 16), (2, 16)))
    conv_weight = jnp.clip(jax.random.uniform(key_of[3], (CONV, DI), jnp.float32, -0.5, 0.5) * block_scale(key_of[3], (CONV, DI), ((1, 16),), -0.4, 0.0), -0.5, 0.5)
    conv_bias = jnp.clip(jax.random.uniform(key_of[4], (DI,), jnp.float32, -0.5, 0.5) * block_scale(key_of[4], (DI,), ((0, 16),), -0.4, 0.0), -0.5, 0.5)
    proj_weight = centred(key_of[5], (DI, RANK + 2 * STATE), DI ** -0.5, 0.0625, ((0, 16),))
    step_weight = centred(key_of[6], (RANK, DI), (3.0 / RANK ** 0.5), 1.0, ((1, 16),))
    step_bias = jnp.clip(-5.0 + 4.0 * jax.random.uniform(key_of[7], (DI,), jnp.float32) ** block_scale(key_of[7], (DI,), ((0, 16),), -0.2, 0.2), -5.0, -1.0)
    decay_log = jnp.clip(-6.0 + 8.7 * jax.random.uniform(key_of[8], (DI, STATE), jnp.float32) ** block_scale(key_of[8], (DI, STATE), ((0, 16),), -0.2, 0.2), -6.0, 2.7)
    skip_gain = jnp.clip(0.5 + 1.0 * jax.random.uniform(key_of[9], (DI,), jnp.float32) ** block_scale(key_of[9], (DI,), ((0, 16),), -0.2, 0.2), 0.5, 1.5)
    out_weight = centred(key_of[10], (DI, D), DI ** -0.5, 0.0625, ((0, 16), (1, 16)))
    moe_gain = jnp.clip(1.0 + 0.15 * jax.random.normal(key_of[11], (D,), jnp.float32), 0.25, 1.75)
    router_weight = centred(key_of[12], (D, EXPERTS), D ** -0.5, 0.09375)
    routes_keys = jax.random.split(jax.random.fold_in(key_of[13], 1), TOKENS // BLOCK)
    routes_turns = jax.random.permutation(jax.random.fold_in(key_of[13], 3), TOKENS // BLOCK)
    routes = jax.vmap(lambda own, number: shared_out(jax.random.fold_in(key_of[13], 2), own, number, BLOCK, EXPERTS, 2, MOST, 2))(routes_keys, routes_turns).reshape((TOKENS, 2))
    gate_weight = centred(key_of[14], (EXPERTS, D, FF), D ** -0.5, 0.09375, ((0, 16), (2, 16)))
    up_weight = centred(key_of[15], (EXPERTS, D, FF), D ** -0.5, 0.09375, ((0, 16), (2, 16)))
    down_weight = centred(key_of[16], (EXPERTS, FF, D), FF ** -0.5, 0.0625, ((0, 16), (1, 16)))
    return {"tokens": tokens, "norm_gain": norm_gain, "in_weight": in_weight, "conv_weight": conv_weight, "conv_bias": conv_bias, "proj_weight": proj_weight, "step_weight": step_weight, "step_bias": step_bias, "decay_log": decay_log, "skip_gain": skip_gain, "out_weight": out_weight, "moe_gain": moe_gain, "router_weight": router_weight, "routes": routes, "gate_weight": gate_weight, "up_weight": up_weight, "down_weight": down_weight}


EPSILON = 1e-06

def rms_norm(values_in, gain_row):
    as_float = values_in.astype(jnp.float32)
    inverse = lax.rsqrt(lax.optimization_barrier(jnp.mean(as_float * as_float, axis=-1, keepdims=True)) + EPSILON)
    return (as_float * inverse * gain_row).astype(jnp.bfloat16)

def scan_pairs(former, latter):
    return (former[0] * latter[0], latter[0] * former[1] + latter[1])

def route_tables(routes, logits, experts, block_rows, most_slots):
    expert_ids = lax.broadcasted_iota(jnp.int32, (1, 1, experts), 2)
    matches = routes[:, :, None] == expert_ids
    picked = lax.optimization_barrier(jnp.sum(jnp.where(matches, logits[:, None, :], 0.0), axis=2))
    first_share = jax.nn.sigmoid(picked[:, 0] - picked[:, 1])
    shares = jnp.stack([first_share, 1.0 - first_share], axis=1)
    weight_table = lax.optimization_barrier(jnp.sum(jnp.where(matches, shares[:, :, None], 0.0), axis=1))
    counts = lax.optimization_barrier(jnp.sum(matches.astype(jnp.int32), axis=1)).astype(jnp.int32)
    blocked = counts.reshape(-1, block_rows, experts)
    before = (jnp.cumsum(blocked, axis=1) - blocked).astype(jnp.int32)
    slot_ids = lax.broadcasted_iota(jnp.int32, (1, 1, 1, most_slots), 3)
    chosen = (blocked[..., None] > 0) & (before[..., None] == slot_ids)
    slot_table = jnp.where(chosen, 1.0, 0.0).astype(jnp.float32)
    return (slot_table, weight_table.reshape(-1, block_rows, experts))

def mixer_scan(step_size, drive_in, input_map, output_map, decay_rate):
    length = step_size.shape[0]
    blocks = length // TOK_SEQ

    def advance(carried, block_in):
        step_block, drive_block, input_block, output_block = block_in
        decay_step = jnp.exp(step_block[:, :, None] * decay_rate[None])
        inject = (step_block * drive_block)[:, :, None] * input_block[:, None, :]
        cumulated, local_state = lax.associative_scan(scan_pairs, (decay_step, inject), axis=0)
        states = local_state + cumulated * carried[None]
        return (states[-1], jnp.einsum('tcn,tn->tc', states, output_block))
    initial = jnp.zeros((DI, STATE), jnp.float32)
    inputs = (step_size.reshape(blocks, TOK_SEQ, DI), drive_in.reshape(blocks, TOK_SEQ, DI), input_map.reshape(blocks, TOK_SEQ, STATE), output_map.reshape(blocks, TOK_SEQ, STATE))
    final_state, outputs = lax.scan(advance, initial, inputs)
    return outputs.reshape(length, DI)

def reference(tokens, norm_gain, in_weight, conv_weight, conv_bias, proj_weight, step_weight, step_bias, decay_log, skip_gain, out_weight, moe_gain, router_weight, routes, gate_weight, up_weight, down_weight):
    length = tokens.shape[0]
    normed = rms_norm(tokens, norm_gain)
    projected = jnp.dot(normed, in_weight.reshape(D, 2 * DI), preferred_element_type=jnp.float32).astype(jnp.bfloat16)
    mixer_in = projected[:, :DI].astype(jnp.float32)
    gate_in = projected[:, DI:].astype(jnp.float32)
    padded = jnp.pad(mixer_in, ((CONV - 1, 0), (0, 0)))
    convolved = conv_bias + jnp.zeros((length, DI), jnp.float32)
    for tap_index in range(CONV):
        convolved = convolved + conv_weight[tap_index] * padded[tap_index:tap_index + length]
    activated = jax.nn.silu(convolved).astype(jnp.bfloat16)
    features = jnp.dot(activated, proj_weight, preferred_element_type=jnp.float32)
    low_rank = features[:, :RANK].astype(jnp.bfloat16)
    input_map = features[:, RANK:RANK + STATE]
    output_map = features[:, RANK + STATE:]
    step_size = jax.nn.softplus(jnp.dot(low_rank, step_weight, preferred_element_type=jnp.float32) + step_bias)
    decay_rate = -jnp.exp(decay_log)
    drive_in = activated.astype(jnp.float32)
    scanned = mixer_scan(step_size, drive_in, input_map, output_map, decay_rate)
    gated_out = ((scanned + skip_gain * drive_in) * jax.nn.silu(gate_in)).astype(jnp.bfloat16)
    mamba_out = jnp.dot(gated_out, out_weight, preferred_element_type=jnp.float32)
    hidden_state = (tokens.astype(jnp.float32) + mamba_out).astype(jnp.bfloat16)
    moe_in = rms_norm(hidden_state, moe_gain)
    logits = jnp.dot(moe_in, router_weight, preferred_element_type=jnp.float32)
    slot_table, weight_table = route_tables(routes, logits, EXPERTS, BLOCK, MOST)
    slotted = jnp.einsum('btem,btd->ebmd', slot_table, moe_in.reshape(-1, BLOCK, D).astype(jnp.float32)).astype(jnp.bfloat16)
    shard_width = FF // N_SEQ

    def one_expert(operands):
        rows_in, gate_mat, up_mat, down_mat = operands
        flat_rows = rows_in.reshape(-1, D)
        gate_act = jnp.dot(flat_rows, gate_mat, preferred_element_type=jnp.float32)
        up_act = jnp.dot(flat_rows, up_mat, preferred_element_type=jnp.float32)
        hidden = (jax.nn.silu(gate_act) * up_act).astype(jnp.bfloat16)
        running = jnp.zeros((flat_rows.shape[0], D), jnp.float32)
        for shard_index in range(N_SEQ):
            lower_edge = shard_index * shard_width
            partial_value = jnp.dot(hidden[:, lower_edge:lower_edge + shard_width], down_mat[lower_edge:lower_edge + shard_width], preferred_element_type=jnp.float32).astype(jnp.bfloat16)
            partial_value = lax.optimization_barrier(partial_value)
            running = running + partial_value.astype(jnp.float32)
        return running.astype(jnp.bfloat16).reshape(rows_in.shape)
    expert_out = lax.map(one_expert, (slotted, gate_weight, up_weight, down_weight))
    mixed_weights = slot_table * weight_table[..., None]
    moe_out = jnp.einsum('btem,ebmd->btd', mixed_weights, expert_out.astype(jnp.float32)).reshape(length, D)
    return (hidden_state.astype(jnp.float32) + moe_out).astype(jnp.bfloat16)
```

```python
import types

import jax
import jax.numpy as jnp
from jax import lax
from jax.experimental import pallas as pl
from jax.experimental.pallas import tpu as pltpu
from jax.sharding import Mesh
from jax.sharding import PartitionSpec as P

SEQ = ("seq_0", "seq_1")
SEQ_EXPERT = ("seq_0", "seq_1", "expert")
EPSILON = 1e-06
F32 = jnp.float32
BF16 = jnp.bfloat16

D = 4096
T = 128
C = 512
FD = 256
N = 16
RANK = 256
HU = 448
ROWS = 32


def mod(v, n):
    return lax.rem(v, n)


def rcopy(src, dst, send, recv, device):
    return pltpu.make_async_remote_copy(
        src_ref=src,
        dst_ref=dst,
        send_sem=send,
        recv_sem=recv,
        device_id=device,
        device_id_type=pl.DeviceIdType.MESH,
    )


def silu(v):
    return v / (1.0 + jnp.exp(-v))


class RingGather:
    def __init__(self, buf, base, half, pos, dev, send, recv):
        self.buf, self.base, self.half, self.dev = buf, base, half, dev
        self.send, self.recv = send, recv
        self.pos, self.right, self.left, self.opp = pos, mod(pos + 1, 4), mod(pos + 3, 4), mod(pos + 2, 4)
        self.started = []

    def part(self, pos, h):
        return self.buf.at[pl.ds(self.base(pos) + h * self.half, self.half)]

    def go(self, pos, h, to, k):
        block = self.part(pos, h)
        copy = rcopy(block, block, self.send.at[k], self.recv.at[k], self.dev(to))
        copy.start()
        self.started.append(copy)

    def arrived(self, pos, h, k):
        block = self.part(pos, h)
        rcopy(block, block, self.send.at[k], self.recv.at[k], self.dev(self.right)).wait_recv()

    def start(self):
        self.go(self.pos, 0, self.right, 0)
        self.go(self.pos, 1, self.left, 3)
        self.go(self.pos, 1, self.right, 1)
        self.go(self.pos, 0, self.left, 2)

    def forward(self):
        self.arrived(self.left, 0, 0)
        self.go(self.left, 0, self.right, 4)
        self.arrived(self.right, 1, 3)
        self.go(self.right, 1, self.left, 5)

    def sides(self):
        self.arrived(self.left, 1, 1)
        self.arrived(self.right, 0, 2)

    def opposite(self):
        self.arrived(self.opp, 0, 4)
        self.arrived(self.opp, 1, 5)

    def drain(self):
        for copy in self.started:
            copy.wait_send()


class RingReduce:
    def __init__(self, part, base, half, pos, dev, first, second, summed, send, recv):
        self.buf, self.base, self.half, self.dev = part, base, half, dev
        self.first, self.second, self.summed = first, second, summed
        self.send, self.recv = send, recv
        self.pos, self.right, self.left, self.opp = pos, mod(pos + 1, 4), mod(pos + 3, 4), mod(pos + 2, 4)
        self.started = []

    def part(self, pos, h):
        return self.buf.at[pl.ds(self.base(pos) + h * self.half, self.half)]

    def go(self, src, dst, to, k):
        copy = rcopy(src, dst, self.send.at[k], self.recv.at[k], self.dev(to))
        copy.start()
        self.started.append(copy)

    def arrived(self, dst, k):
        rcopy(dst, dst, self.send.at[k], self.recv.at[k], self.dev(self.right)).wait_recv()

    def start(self):
        h = self.half
        self.go(self.part(self.opp, 0), self.first.at[0], self.right, 0)
        self.go(self.part(self.opp, 1), self.first.at[1], self.left, 1)
        self.go(self.part(self.right, 1), self.second.at[0, pl.ds(h, h)], self.right, 2)
        self.go(self.part(self.left, 0), self.second.at[1, pl.ds(0, h)], self.left, 3)

    def middle(self):
        h = self.half
        for side, (owner, which) in enumerate(((self.right, 0), (self.left, 1))):
            self.arrived(self.first.at[side], side)
            at = self.base(owner) + which * h

            @pl.loop(0, h)
            def _(i):
                total = self.buf[at + i].astype(F32) + self.first[side, i].astype(F32)
                self.summed[side, i] = total.astype(BF16)

            self.go(self.summed.at[side], self.second.at[side, pl.ds(which * h, h)], owner, 4 + side)

    def finish(self, store):
        h = self.half
        self.arrived(self.second.at[0, pl.ds(h, h)], 2)
        self.arrived(self.second.at[1, pl.ds(0, h)], 3)
        self.arrived(self.second.at[0, pl.ds(0, h)], 4)
        self.arrived(self.second.at[1, pl.ds(h, h)], 5)
        at = self.base(self.pos)

        @pl.loop(0, 2 * h)
        def _(i):
            total = self.buf[at + i].astype(F32) + self.second[0, i].astype(F32)
            store(i, (total + self.second[1, i].astype(F32)).astype(BF16))

    def drain(self):
        for copy in self.started:
            copy.wait_send()


INPUTS = (
    ("tokens", "v"), ("norm_gain", "v"), ("in_weight", "a"), ("conv_weight", "v"), ("conv_bias", "v"),
    ("proj_weight", "v"), ("step_weight", "v"), ("step_bias", "v"), ("decay_log", "v"), ("skip_gain", "v"),
    ("out_weight", "a"), ("moe_gain", "v"), ("router_weight", "v"), ("routes", "v"), ("routes_t", "v"),
    ("gate_weight", "a"), ("up_weight", "a"), ("down_weight", "a"),
)

SCRATCH = {
    "normed": ((16, T, FD), BF16),
    "tok_g": ((16, T, FD), BF16),
    "wg": ((8, FD // 2, 2 * C), BF16),
    "part": ((4, T, 2 * C), BF16),
    "own_part": ((T, 2 * C), F32),
    "rs_recv": ((4, T, 2 * C), BF16),
    "padf": ((T + 16, C), F32),
    "gate": ((T, C), F32),
    "hsrc": ((16, C), BF16),
    "hdst": ((16, C), BF16),
    "act": ((T, C), BF16),
    "feat": ((16, 8, 384), F32),
    "frecv": ((16, 8, 384), F32),
    "fsum": ((8, 384), F32),
    "fall": ((16, 8, 384), F32),
    "step": ((T, C), F32),
    "drive": ((T, C), F32),
    "maps_t": ((ROWS, T), F32),
    "y": ((T, C), F32),
    "stx": ((24, C), F32),
    "stall": ((16, 24, C), F32),
    "gated": ((T, C), BF16),
    "ow": ((32, C // 2, FD), BF16),
    "outp": ((16, 8, D), BF16),
    "pair": ((8, 8, D), BF16),
    "zs": ((8, 8, D), BF16),
    "zrecv": ((8, 8, D), BF16),
    "hid": ((8, D), F32),
    "wt": ((8, ROWS), F32),
    "slots": ((ROWS, D), F32),
    "out3": ((16, 2, D), BF16),
    "in3": ((16, 2, D), BF16),
    "rows": ((32, 16, D), BF16),
    "gw": ((D, HU), BF16),
    "uw": ((D, HU), BF16),
    "dw": ((HU, D), BF16),
    "acc_g": ((T, HU), F32),
    "acc_u": ((T, HU), F32),
    "hidden": ((T, HU), BF16),
    "ypart": ((32, 16, D), BF16),
    "r1": ((2, 4, 16, D), BF16),
    "r2": ((2, 8, 16, D), BF16),
    "sm": ((2, 4, 16, D), BF16),
    "zin": ((8, 16, D), BF16),
    "q1": ((2, 1, 16, D), BF16),
    "q2": ((2, 2, 16, D), BF16),
    "qm": ((2, 1, 16, D), BF16),
    "ret3": ((16, 2, D), BF16),
    "back3": ((16, 2, D), BF16),
}

SEMS = {
    "local": 5,
    "tok": 4, "win": 6, "rs": 4, "halo": 1, "f1": 16, "f2": 16, "st": 16, "ow1": 6, "ow2": 6,
    "pair": 1, "z": 8, "disp": 16, "ag1": 6, "ag2": 6, "red1": 6, "red2": 6, "ret": 16,
}

FAR_16 = (8, 7, 9, 6, 10, 5, 11, 4, 12, 3, 13, 2, 14, 1, 15)
FAR_8 = (4, 3, 5, 2, 6, 1, 7)


def kernel(*refs):
    count = len(INPUTS)
    I = types.SimpleNamespace(**{name: r for (name, _), r in zip(INPUTS, refs[:count])})
    out_ref = refs[count]
    rest = refs[count + 1 :]
    S = types.SimpleNamespace(**dict(zip(SCRATCH, rest[: len(SCRATCH)])))
    rest = rest[len(SCRATCH) :]
    sem_s = dict(zip(SEMS, rest[: len(SEMS)]))
    sem_r = dict(zip(SEMS, rest[len(SEMS) :]))

    x, y, e = lax.axis_index("seq_0"), lax.axis_index("seq_1"), lax.axis_index("expert")
    c, z = mod(e, 2), e // 2
    s = 4 * x + y
    a = c * x + (1 - c) * y
    b = (1 - c) * x + c * y

    def dev_a(k):
        return (x + c * (k - x), y + (1 - c) * (k - y), e)

    def dev_b(k):
        return (x + (1 - c) * (k - x), y + c * (k - y), e)

    def dev_s(k):
        return (k // 4, mod(k, 4), e)

    def shard_of(k, q):
        return c * (4 * k + q) + (1 - c) * (4 * q + k)

    drains = []

    def finish_later(copy):
        copy.start()
        drains.append(copy)

    barrier = pltpu.get_barrier_semaphore()
    for d in range(1, 16):
        pl.semaphore_signal(barrier, inc=1, device_id=(x, y, mod(e + d, 16)), device_id_type=pl.DeviceIdType.MESH)
        pl.semaphore_signal(barrier, inc=1, device_id=dev_s(mod(s + d, 16)), device_id_type=pl.DeviceIdType.MESH)

    own = b * 4 + a
    local = [
        pltpu.make_async_copy(I.in_weight, S.wg.at[pl.ds(2 * b, 2)], sem_s["local"].at[0]),
        pltpu.make_async_copy(I.out_weight, S.ow.at[pl.ds(2 * own, 2)], sem_s["local"].at[1]),
        pltpu.make_async_copy(I.gate_weight, S.gw, sem_s["local"].at[2]),
        pltpu.make_async_copy(I.up_weight, S.uw, sem_s["local"].at[3]),
        pltpu.make_async_copy(I.down_weight, S.dw, sem_s["local"].at[4]),
    ]
    for copy in local:
        copy.start()

    gain = I.norm_gain[...]

    @pl.loop(0, T // 16)
    def _(i):
        rows = pl.ds(pl.multiple_of(i * 16, 16), 16)
        v = I.tokens[rows, :].astype(F32)
        inverse = lax.rsqrt(jnp.mean(v * v, axis=-1, keepdims=True) + EPSILON)
        normed = (v * inverse * gain).astype(BF16)
        for j in range(16):
            k = (1 - c) * (j % 4) + c * (j // 4)
            q = (1 - c) * (j // 4) + c * (j % 4)
            S.normed[4 * k + q, rows, :] = normed[:, j * FD : (j + 1) * FD]

    pl.semaphore_wait(barrier, 30)

    local[0].wait()
    win = RingGather(S.wg, lambda p: 2 * p, 1, b, dev_b, sem_s["win"], sem_r["win"])
    win.start()
    for d in (2, 1, 3):
        k = mod(a + d, 4)
        finish_later(
            rcopy(
                S.normed.at[pl.ds(4 * k, 4)], S.tok_g.at[pl.ds(4 * a, 4)],
                sem_s["tok"].at[d], sem_r["tok"].at[d], dev_a(k),
            )
        )
    win.forward()
    win.sides()
    win.opposite()
    for d in (2, 1, 3):
        block = S.tok_g.at[pl.ds(4 * mod(a + 4 - d, 4), 4)]
        rcopy(block, block, sem_s["tok"].at[d], sem_r["tok"].at[d], dev_a(mod(a + 1, 4))).wait_recv()
    for d in (2, 1, 3, 0):
        k = mod(a + d, 4)
        source = S.tok_g if d else S.normed

        @pl.loop(0, 2 * C // 256)
        def _(n):
            cols = pl.ds(pl.multiple_of(n * 256, 256), 256)
            total = jnp.zeros((T, 256), F32)
            for q in range(4):
                weight = S.wg[2 * q : 2 * q + 2, :, cols].reshape(FD, 256)
                total = total + jnp.dot(source[4 * k + q], weight, preferred_element_type=F32)
            if d:
                S.part[k, :, cols] = total.astype(BF16)
            else:
                S.own_part[:, cols] = total

        if d:
            finish_later(
                rcopy(S.part.at[k], S.rs_recv.at[a], sem_s["rs"].at[d], sem_r["rs"].at[d], dev_a(k))
            )

    local[1].wait()
    ow1 = RingGather(S.ow, lambda p: (b * 4 + p) * 2, 1, a, dev_a, sem_s["ow1"], sem_r["ow1"])
    ow1.start()

    for d in (2, 1, 3):
        block = S.rs_recv.at[mod(a + 4 - d, 4)]
        rcopy(block, block, sem_s["rs"].at[d], sem_r["rs"].at[d], dev_a(mod(a + 1, 4))).wait_recv()

    @pl.loop(0, T // 16)
    def _(i):
        rows = pl.ds(pl.multiple_of(i * 16, 16), 16)
        total = S.own_part[rows, :]
        for d in (1, 2, 3):
            total = total + S.rs_recv[mod(a + d, 4), rows, :].astype(F32)
        total = total.astype(BF16).astype(F32)
        S.padf[pl.ds(pl.multiple_of(16 + i * 16, 16), 16), :] = total[:, :C]
        S.gate[rows, :] = total[:, C:]

    S.hsrc[...] = S.padf[T : T + 16, :].astype(BF16)
    finish_later(
        rcopy(S.hsrc, S.hdst, sem_s["halo"].at[0], sem_r["halo"].at[0], dev_s(mod(s + 1, 16)))
    )
    ow1.forward()
    rcopy(S.hdst, S.hdst, sem_s["halo"].at[0], sem_r["halo"].at[0], dev_s(mod(s + 1, 16))).wait_recv()
    first = jnp.zeros((16, C), jnp.int32) + s
    S.padf[0:16, :] = jnp.where(first > 0, S.hdst[...].astype(F32), 0.0)

    @pl.loop(0, T // 16)
    def _(i):
        window = S.padf[pl.ds(pl.multiple_of(i * 16, 16), 32), :]
        total = I.conv_bias[...] + jnp.zeros((16, C), F32)
        for tap in range(4):
            total = total + I.conv_weight[tap : tap + 1, :] * window[13 + tap : 29 + tap, :]
        S.act[pl.ds(pl.multiple_of(i * 16, 16), 16), :] = silu(total).astype(BF16)

    full = jnp.dot(S.act[...], I.proj_weight[...], preferred_element_type=F32)
    S.feat[:, :, RANK:] = jnp.zeros((16, 8, 128), F32)
    S.feat[:, :, :RANK] = full[:, :RANK].reshape(16, 8, RANK)
    S.feat[:, :, RANK : RANK + 2 * N] = full[:, RANK:].reshape(16, 8, 2 * N)
    for d in FAR_16:
        to = mod(e + d, 16)
        finish_later(rcopy(S.feat.at[to], S.frecv.at[e], sem_s["f1"].at[d], sem_r["f1"].at[d], (x, y, to)))
    ow1.sides()
    ow1.opposite()
    ow2 = RingGather(S.ow, lambda p: p * 8, 4, b, dev_b, sem_s["ow2"], sem_r["ow2"])
    ow2.start()
    total = S.feat[e]
    for d in range(1, 16):
        block = S.frecv.at[mod(e + 16 - d, 16)]
        rcopy(block, block, sem_s["f1"].at[d], sem_r["f1"].at[d], (x, y, mod(e + 1, 16))).wait_recv()
    for d in range(1, 16):
        total = total + S.frecv[mod(e + d, 16)]
    S.fsum[...] = total
    for d in FAR_16:
        to = mod(e + d, 16)
        finish_later(rcopy(S.fsum, S.fall.at[e], sem_s["f2"].at[d], sem_r["f2"].at[d], (x, y, to)))
    S.fall[e] = total
    for d in range(1, 16):
        block = S.fall.at[mod(e + 16 - d, 16)]
        rcopy(block, block, sem_s["f2"].at[d], sem_r["f2"].at[d], (x, y, mod(e + 1, 16))).wait_recv()
    low = S.fall[:, :, :RANK].reshape(T, RANK).astype(BF16)
    S.maps_t[...] = jnp.transpose(S.fall[:, :, RANK:].reshape(T, 128))[: 2 * N, :]
    raw = jnp.dot(low, I.step_weight[...], preferred_element_type=F32) + I.step_bias[...]
    S.step[...] = jnp.maximum(raw, 0.0) + jnp.log1p(jnp.exp(-jnp.abs(raw)))
    S.drive[...] = S.step[...] * S.act[...].astype(F32)

    rate = -jnp.exp(I.decay_log[...])

    def scan(start, emit):
        def block(i, state):
            rows = pl.ds(pl.multiple_of(i * 8, 8), 8)
            steps, drives = S.step[rows, :], S.drive[rows, :]
            maps = pltpu.roll(S.maps_t[...], mod(T - 8 * i, T), 1)
            lines = []
            for t in range(8):
                state = jnp.exp(steps[t : t + 1, :] * rate) * state + drives[t : t + 1, :] * maps[:N, t : t + 1]
                if emit:
                    lines.append(jnp.sum(state * maps[N:, t : t + 1], axis=0, keepdims=True))
            if emit:
                S.y[rows, :] = jnp.concatenate(lines, axis=0)
            return state

        return lax.fori_loop(0, T // 8, block, start)

    zero_state = jnp.zeros((N, C), F32)
    S.stx[0:N, :] = scan(zero_state, False)
    S.stx[N : N + 8, :] = jnp.broadcast_to(jnp.sum(S.step[...], axis=0, keepdims=True), (8, C))

    def state_copy(d):
        return rcopy(
            S.stx, S.stall.at[s], sem_s["st"].at[d], sem_r["st"].at[d], dev_s(mod(s + d, 16))
        )

    for d in range(15, 0, -1):

        @pl.when(s + d < 16)
        def _():
            state_copy(d).start()

    ow2.forward()
    for d in range(1, 16):

        @pl.when(s - d >= 0)
        def _():
            block = S.stall.at[mod(s + 16 - d, 16)]
            rcopy(block, block, sem_s["st"].at[d], sem_r["st"].at[d], dev_s(mod(s + d, 16))).wait_recv()

    def compose(k, state):
        return jnp.exp(rate * S.stall[k, N : N + 1, :]) * state + S.stall[k, 0:N, :]

    scan(lax.fori_loop(0, s, compose, zero_state), True)

    @pl.loop(0, T // 16)
    def _(i):
        rows = pl.ds(pl.multiple_of(i * 16, 16), 16)
        scanned = S.y[rows, :] + I.skip_gain[...] * S.act[rows, :].astype(F32)
        S.gated[rows, :] = (scanned * silu(S.gate[rows, :])).astype(BF16)

    ow2.sides()
    ow2.opposite()

    @pl.loop(0, 16)
    def _(u):
        column = shard_of(mod(u, 4), u // 4)
        weight = S.ow[pl.ds(2 * u, 2)].reshape(C, FD)
        total = jnp.dot(S.gated[...], weight, preferred_element_type=F32).reshape(8, 2, 8, FD)
        cols = pl.ds(pl.multiple_of(column * FD, FD), FD)
        S.outp[0:8, :, cols] = total[:, 0].astype(BF16)
        S.outp[8:16, :, cols] = total[:, 1].astype(BF16)

    other = e + 1 - 2 * c
    pair = rcopy(S.outp.at[pl.ds(8 * (1 - c), 8)], S.pair, sem_s["pair"].at[0], sem_r["pair"].at[0], (x, y, other))
    finish_later(pair)
    pair.wait_recv()
    for d in FAR_8:
        zz = mod(z + d, 8)
        S.zs[zz] = (S.outp[8 * c + zz].astype(F32) + S.pair[zz].astype(F32)).astype(BF16)
        finish_later(
            rcopy(S.zs.at[zz], S.zrecv.at[z], sem_s["z"].at[d], sem_r["z"].at[d], (x, y, 2 * zz + c))
        )
    total = S.outp[8 * c + z].astype(F32) + S.pair[z].astype(F32)
    for d in range(1, 8):
        block = S.zrecv.at[mod(z + 8 - d, 8)]
        rcopy(block, block, sem_s["z"].at[d], sem_r["z"].at[d], (x, y, other)).wait_recv()
    for d in range(1, 8):
        total = total + S.zrecv[mod(z + d, 8)].astype(F32)

    both = I.tokens[pl.ds(pl.multiple_of(16 * z, 16), 16), :].astype(F32)
    core = jnp.zeros((8, D), jnp.int32) + c
    mine = jnp.where(core == 0, both[:8, :], both[8:, :])
    hid = (mine + total).astype(BF16).astype(F32)
    S.hid[...] = hid
    inverse = lax.rsqrt(jnp.mean(hid * hid, axis=-1, keepdims=True) + EPSILON)
    moe_in = (hid * inverse * I.moe_gain[...]).astype(BF16).astype(F32)
    twice = jnp.concatenate([moe_in, moe_in], axis=0).astype(BF16)
    logits = jnp.dot(twice, I.router_weight[...], preferred_element_type=F32)[:8, :]

    ids = lax.broadcasted_iota(jnp.int32, (8, 16), 1)
    route_a, route_b = I.routes[:, 0:1], I.routes[:, 1:2]
    picked_a = jnp.sum(jnp.where(route_a == ids, logits, 0.0), axis=1, keepdims=True)
    picked_b = jnp.sum(jnp.where(route_b == ids, logits, 0.0), axis=1, keepdims=True)
    share_a = 1.0 / (1.0 + jnp.exp(picked_b - picked_a))
    share_b = 1.0 - share_a

    def chosen(slot, token, ra, rb, row_of):
        expert, slot_no = slot // 2, mod(slot, 2)
        match_a = jnp.where(ra == expert, 1.0, 0.0)
        match_b = jnp.where(rb == expert, 1.0, 0.0)
        named = match_a + match_b
        before = jnp.zeros_like(named)
        for t in range(7):
            before = before + jnp.where(token > t, row_of(named, t), 0.0)
        hit = jnp.where(before == slot_no.astype(F32), named, 0.0)
        return hit, match_a, match_b

    hit, match_a, match_b = chosen(
        lax.broadcasted_iota(jnp.int32, (8, ROWS), 1), lax.broadcasted_iota(jnp.int32, (8, ROWS), 0),
        route_a, route_b, lambda v, t: v[t : t + 1, :],
    )
    S.wt[...] = hit * (match_a * share_a + match_b * share_b)
    hit_t, _, _ = chosen(
        lax.broadcasted_iota(jnp.int32, (ROWS, 8), 0), lax.broadcasted_iota(jnp.int32, (ROWS, 8), 1),
        I.routes_t[0:1, :], I.routes_t[1:2, :], lambda v, t: v[:, t : t + 1],
    )
    for n in range(D // 512):
        cols = slice(n * 512, n * 512 + 512)
        slotted = jnp.zeros((ROWS, 512), F32)
        for t in range(8):
            slotted = slotted + hit_t[:, t : t + 1] * moe_in[t : t + 1, cols]
        S.slots[:, cols] = slotted
    for i in range(16):
        S.out3[i] = S.slots[2 * i : 2 * i + 2, :].astype(BF16)

    for d in FAR_16:
        to = mod(e + d, 16)
        finish_later(rcopy(S.out3.at[to], S.in3.at[e], sem_s["disp"].at[d], sem_r["disp"].at[d], (x, y, to)))
    S.in3[e] = S.out3[e]
    for d in range(1, 16):
        block = S.in3.at[mod(e + 16 - d, 16)]
        rcopy(block, block, sem_s["disp"].at[d], sem_r["disp"].at[d], (x, y, mod(e + 1, 16))).wait_recv()
    for i in range(16):
        S.slots[2 * i : 2 * i + 2, :] = S.in3[i].astype(F32)
    for h in range(2):
        S.rows[2 * own + h] = S.slots[16 * h : 16 * h + 16, :].astype(BF16)
    ag1 = RingGather(S.rows, lambda p: (b * 4 + p) * 2, 1, a, dev_a, sem_s["ag1"], sem_r["ag1"])
    ag1.start()
    ag1.forward()
    ag1.sides()
    ag1.opposite()
    ag2 = RingGather(S.rows, lambda p: p * 8, 4, b, dev_b, sem_s["ag2"], sem_r["ag2"])
    ag2.start()
    for copy in local[2:]:
        copy.wait()

    def experts(p):
        S.acc_g[...] = jnp.zeros((T, HU), F32)
        S.acc_u[...] = jnp.zeros((T, HU), F32)

        @pl.loop(0, D // 512)
        def _(n):
            cols = pl.ds(pl.multiple_of(n * 512, 512), 512)
            rows = S.rows[pl.ds(8 * p, 8), :, cols].reshape(T, 512)
            S.acc_g[...] += jnp.dot(rows, S.gw[cols, :], preferred_element_type=F32)
            S.acc_u[...] += jnp.dot(rows, S.uw[cols, :], preferred_element_type=F32)

        S.hidden[...] = (silu(S.acc_g[...]) * S.acc_u[...]).astype(BF16)

        @pl.loop(0, D // 512)
        def _(n):
            cols = pl.ds(pl.multiple_of(n * 512, 512), 512)
            result = jnp.dot(S.hidden[...], S.dw[:, cols], preferred_element_type=F32)
            S.ypart[pl.ds(8 * p, 8), :, cols] = result.reshape(8, 16, 512).astype(BF16)

    experts(b)
    ag2.forward()
    ag2.sides()
    experts(ag2.left)
    experts(ag2.right)
    ag2.opposite()
    experts(ag2.opp)

    red1 = RingReduce(
        S.ypart, lambda p: p * 8, 4, b, dev_b, S.r1, S.r2, S.sm, sem_s["red1"], sem_r["red1"]
    )
    red1.start()
    red1.middle()

    def to_second(i, value):
        S.zin[i] = value

    red1.finish(to_second)
    red2 = RingReduce(
        S.zin, lambda p: p * 2, 1, a, dev_a, S.q1, S.q2, S.qm, sem_s["red2"], sem_r["red2"]
    )
    red2.start()
    red2.middle()

    def to_slots(i, value):
        S.slots[pl.ds(pl.multiple_of(16 * i, 16), 16), :] = value.astype(F32)

    red2.finish(to_slots)
    for i in range(16):
        S.ret3[i] = S.slots[2 * i : 2 * i + 2, :].astype(BF16)
    for d in FAR_16:
        to = mod(e + d, 16)
        finish_later(rcopy(S.ret3.at[to], S.back3.at[e], sem_s["ret"].at[d], sem_r["ret"].at[d], (x, y, to)))
    S.back3[e] = S.ret3[e]
    for d in range(1, 16):
        block = S.back3.at[mod(e + 16 - d, 16)]
        rcopy(block, block, sem_s["ret"].at[d], sem_r["ret"].at[d], (x, y, mod(e + 1, 16))).wait_recv()

    mixed = S.hid[...]
    weights = S.wt[...]
    for i in range(16):
        pair_rows = S.back3[i].astype(F32)
        for m in range(2):
            j = 2 * i + m
            mixed = mixed + weights[:, j : j + 1] * pair_rows[m : m + 1, :]
    out_ref[...] = mixed.astype(BF16)

    for copy in drains:
        copy.wait_send()
    for ring in (win, ow1, ow2, ag1, ag2, red1, red2):
        ring.drain()
    for d in range(1, 16):

        @pl.when(s + d < 16)
        def _():
            state_copy(d).wait_send()


def local_step(
    tokens, norm_gain, in_weight, conv_weight, conv_bias, proj_weight, step_weight, step_bias, decay_log,
    skip_gain, out_weight, moe_gain, router_weight, routes, gate_weight, up_weight, down_weight,
):
    operands = (
        tokens, norm_gain[None], in_weight.reshape(2, FD // 2, 2 * C), conv_weight, conv_bias[None],
        proj_weight, step_weight, step_bias[None], jnp.transpose(decay_log), skip_gain[None],
        out_weight.reshape(2, C // 2, FD), moe_gain[None], router_weight, routes, jnp.transpose(routes),
        gate_weight[0], up_weight[0], down_weight[0],
    )
    spaces = {"v": pltpu.VMEM, "a": pl.ANY}
    return pl.pallas_call(
        kernel,
        out_shape=jax.ShapeDtypeStruct((8, D), BF16),
        in_specs=[pl.BlockSpec(memory_space=spaces[kind]) for _, kind in INPUTS],
        out_specs=pl.BlockSpec(memory_space=pltpu.VMEM),
        scratch_shapes=[pltpu.VMEM(shape, dtype) for shape, dtype in SCRATCH.values()]
        + [pltpu.SemaphoreType.DMA((count,)) for count in SEMS.values()] * 2,
        compiler_params=pltpu.CompilerParams(
            collective_id=0, has_side_effects=True, vmem_limit_bytes=60 * 1024 * 1024
        ),
    )(*operands)


def solution(mesh):
    split = Mesh(mesh.devices.reshape(4, 4, mesh.shape["expert"]), ("seq_0", "seq_1", "expert"))
    in_specs = (
        P(SEQ, None),
        P(),
        P(SEQ, None, "expert"),
        P(None, "expert"),
        P("expert"),
        P("expert", None),
        P(None, "expert"),
        P("expert"),
        P("expert", None),
        P("expert"),
        P("expert", SEQ),
        P(),
        P(),
        P(SEQ_EXPERT, None),
        P("expert", None, SEQ),
        P("expert", None, SEQ),
        P("expert", SEQ, None),
    )
    out_specs = P(SEQ_EXPERT, None)
    return jax.shard_map(local_step, mesh=split, in_specs=in_specs, out_specs=out_specs, check_vma=False)
```

```python
import types

import jax
import jax.numpy as jnp
from jax import lax
from jax.experimental import pallas as pl
from jax.experimental.pallas import tpu as pltpu
from jax.sharding import Mesh
from jax.sharding import PartitionSpec as P

SEQ = ("seq_0", "seq_1")
SEQ_EXPERT = ("seq_0", "seq_1", "expert")
EPSILON = 1e-06
F32 = jnp.float32
BF16 = jnp.bfloat16

D = 4096
T = 128
C = 512
FD = 256
N = 16
RANK = 256
HU = 448
ROWS = 32


def mod(v, n):
    return lax.rem(v, n)


def rcopy(src, dst, send, recv, device):
    return pltpu.make_async_remote_copy(
        src_ref=src,
        dst_ref=dst,
        send_sem=send,
        recv_sem=recv,
        device_id=device,
        device_id_type=pl.DeviceIdType.MESH,
    )


def dot_t(left, right):
    return lax.dot_general(left, right, (((1,), (1,)), ((), ())), preferred_element_type=F32)


def silu(v):
    return v / (1.0 + jnp.exp(-v))


class RingGather:
    def __init__(self, buf, base, half, pos, dev, send, recv, offset=0):
        self.buf, self.base, self.half, self.dev = buf, base, half, dev
        self.send, self.recv, self.offset = send, recv, offset
        self.pos, self.right, self.left, self.opp = pos, mod(pos + 1, 4), mod(pos + 3, 4), mod(pos + 2, 4)
        self.started = []

    def part(self, pos, h):
        return self.buf.at[pl.ds(self.base(pos) + h * self.half, self.half)]

    def go(self, pos, h, to, k):
        block = self.part(pos, h)
        k = k + self.offset
        copy = rcopy(block, block, self.send.at[k], self.recv.at[k], self.dev(to))
        copy.start()
        self.started.append(copy)

    def arrived(self, pos, h, k):
        block = self.part(pos, h)
        k = k + self.offset
        rcopy(block, block, self.send.at[k], self.recv.at[k], self.dev(self.right)).wait_recv()

    def start(self):
        self.go(self.pos, 0, self.right, 0)
        self.go(self.pos, 1, self.left, 3)
        self.go(self.pos, 1, self.right, 1)
        self.go(self.pos, 0, self.left, 2)

    def forward(self):
        self.arrived(self.left, 0, 0)
        self.go(self.left, 0, self.right, 4)
        self.arrived(self.right, 1, 3)
        self.go(self.right, 1, self.left, 5)

    def sides(self):
        self.arrived(self.left, 1, 1)
        self.arrived(self.right, 0, 2)

    def opposite(self):
        self.arrived(self.opp, 0, 4)
        self.arrived(self.opp, 1, 5)

    def drain(self):
        for copy in self.started:
            copy.wait_send()


class RingReduce:
    def __init__(self, part, base, half, pos, dev, first, second, summed, send, recv):
        self.buf, self.base, self.half, self.dev = part, base, half, dev
        self.first, self.second, self.summed = first, second, summed
        self.send, self.recv = send, recv
        self.pos, self.right, self.left, self.opp = pos, mod(pos + 1, 4), mod(pos + 3, 4), mod(pos + 2, 4)
        self.started = []

    def part(self, pos, h):
        return self.buf.at[pl.ds(self.base(pos) + h * self.half, self.half)]

    def go(self, src, dst, to, k):
        copy = rcopy(src, dst, self.send.at[k], self.recv.at[k], self.dev(to))
        copy.start()
        self.started.append(copy)

    def arrived(self, dst, k):
        rcopy(dst, dst, self.send.at[k], self.recv.at[k], self.dev(self.right)).wait_recv()

    def start(self):
        self.go(self.part(self.opp, 0), self.first.at[0], self.right, 0)
        self.go(self.part(self.opp, 1), self.first.at[1], self.left, 1)

    def start_sides(self):
        h = self.half
        self.go(self.part(self.right, 1), self.second.at[0, pl.ds(h, h)], self.right, 2)
        self.go(self.part(self.left, 0), self.second.at[1, pl.ds(0, h)], self.left, 3)

    def middle(self):
        h = self.half
        for side, (owner, which) in enumerate(((self.right, 0), (self.left, 1))):
            self.arrived(self.first.at[side], side)
            at = self.base(owner) + which * h

            @pl.loop(0, h)
            def _(i):
                total = self.buf[at + i].astype(F32) + self.first[side, i].astype(F32)
                self.summed[side, i] = total.astype(BF16)

            self.go(self.summed.at[side], self.second.at[side, pl.ds(which * h, h)], owner, 4 + side)

    def finish(self, store):
        h = self.half
        self.arrived(self.second.at[0, pl.ds(h, h)], 2)
        self.arrived(self.second.at[1, pl.ds(0, h)], 3)
        self.arrived(self.second.at[0, pl.ds(0, h)], 4)
        self.arrived(self.second.at[1, pl.ds(h, h)], 5)
        at = self.base(self.pos)

        @pl.loop(0, 2 * h)
        def _(i):
            total = self.buf[at + i].astype(F32) + self.second[0, i].astype(F32)
            store(i, (total + self.second[1, i].astype(F32)).astype(BF16))

    def drain(self):
        for copy in self.started:
            copy.wait_send()


INPUTS = (
    ("tokens", "v"), ("norm_gain", "v"), ("in_weight", "a"), ("conv_weight", "v"), ("conv_bias", "v"),
    ("proj_weight", "v"), ("step_weight", "v"), ("step_bias", "v"), ("decay_log", "v"), ("skip_gain", "v"),
    ("out_weight", "a"), ("moe_gain", "v"), ("router_weight", "v"), ("routes", "v"),
    ("gate_weight", "a"), ("up_weight", "a"), ("down_weight", "a"),
)

CHUNKS = 4
WIDE = D // CHUNKS

SCRATCH = {
    "normed": ((16, T, FD), BF16),
    "tok_g": ((16, T, FD), BF16),
    "trelay": ((2, 2, T, FD), BF16),
    "wg": ((16, FD // 2, C), BF16),
    "part_0": ((8, T // 2, C), BF16),
    "part_1": ((8, T // 2, C), BF16),
    "m1_0": ((2, 1, T // 2, C), BF16),
    "m2_0": ((2, 2, T // 2, C), BF16),
    "ms_0": ((2, 1, T // 2, C), BF16),
    "m1_1": ((2, 1, T // 2, C), BF16),
    "m2_1": ((2, 2, T // 2, C), BF16),
    "ms_1": ((2, 1, T // 2, C), BF16),
    "padf": ((T + 16, C), F32),
    "gate": ((T, C), F32),
    "hsrc": ((16, C), BF16),
    "hdst": ((16, C), BF16),
    "act": ((T, C), BF16),
    "feat": ((16, 8, 384), BF16),
    "frecv": ((16, 8, 384), BF16),
    "fsum": ((8, 384), BF16),
    "fall": ((16, 8, 384), BF16),
    "step": ((T, C), F32),
    "drive": ((T, C), F32),
    "maps_t": ((ROWS, T), F32),
    "y": ((T, C), F32),
    "stx": ((24, C), F32),
    "stall": ((16, 24, C), F32),
    "gated": ((T, C), BF16),
    "ow": ((32, C // 2, FD), BF16),
    "outp": ((16, 8, D), BF16),
    "pair": ((8, 8, D), BF16),
    "zs": ((8, 8, D), BF16),
    "zrecv": ((8, 8, D), BF16),
    "hid": ((8, D), F32),
    "wt": ((8, ROWS), F32),
    "slots": ((ROWS, D), F32),
    "out3": ((16, 2, D), BF16),
    "in3": ((16, 2, D), BF16),
    "rows": ((32, 16, D), BF16),
    "gw": ((HU, D), BF16),
    "uw": ((HU, D), BF16),
    "dw": ((HU, D), BF16),
    "acc_g": ((2 * T, HU), F32),
    "acc_u": ((2 * T, HU), F32),
    "hidden": ((2 * T, HU), BF16),
    **{
        f"{name}_{chunk}": ((*shape, 16, WIDE), BF16)
        for chunk in range(CHUNKS)
        for name, shape in {
            "y": (32,), "r1": (2, 4), "r2": (2, 8), "sm": (2, 4), "zin": (8,), "q1": (2, 1), "q2": (2, 2), "qm": (2, 1),
        }.items()
    },
    "ret_0": ((16, 2, D // 2), BF16),
    "ret_1": ((16, 2, D // 2), BF16),
    "back_0": ((16, 2, D // 2), BF16),
    "back_1": ((16, 2, D // 2), BF16),
}

SEMS = {
    "local": 6,
    "tok": 6, "win0": 6, "win1": 6, "mix": 6, "gat": 6, "halo": 1, "f1": 16, "f2": 16, "st": 16, "ow1": 6, "ow2": 6,
    "pair": 1, "z": 8, "disp": 16, "ag1": 6, "ag2": 24,
    **{f"{name}_{chunk}": 6 for name in ("red1", "red2") for chunk in range(CHUNKS)},
    "ret_0": 16, "ret_1": 16,
}

FAR_16 = (8, 7, 9, 6, 10, 5, 11, 4, 12, 3, 13, 2, 14, 1, 15)
FAR_8 = (4, 3, 5, 2, 6, 1, 7)


def kernel(*refs):
    count = len(INPUTS)
    I = types.SimpleNamespace(**{name: r for (name, _), r in zip(INPUTS, refs[:count])})
    out_ref = refs[count]
    rest = refs[count + 1 :]
    S = types.SimpleNamespace(**dict(zip(SCRATCH, rest[: len(SCRATCH)])))
    rest = rest[len(SCRATCH) :]
    sem_s = dict(zip(SEMS, rest[: len(SEMS)]))
    sem_r = dict(zip(SEMS, rest[len(SEMS) :]))

    x, y, e = lax.axis_index("seq_0"), lax.axis_index("seq_1"), lax.axis_index("expert")
    c, z = mod(e, 2), e // 2
    s = 4 * x + y
    a = c * x + (1 - c) * y
    b = (1 - c) * x + c * y

    def dev_a(k):
        return (x + c * (k - x), y + (1 - c) * (k - y), e)

    def dev_b(k):
        return (x + (1 - c) * (k - x), y + c * (k - y), e)

    def dev_s(k):
        return (k // 4, mod(k, 4), e)

    def shard_of(k, q):
        return c * (4 * k + q) + (1 - c) * (4 * q + k)

    drains = []

    def finish_later(copy):
        copy.start()
        drains.append(copy)

    barrier = pltpu.get_barrier_semaphore()
    for d in range(1, 16):
        pl.semaphore_signal(barrier, inc=1, device_id=(x, y, mod(e + d, 16)), device_id_type=pl.DeviceIdType.MESH)
        pl.semaphore_signal(barrier, inc=1, device_id=dev_s(mod(s + d, 16)), device_id_type=pl.DeviceIdType.MESH)

    own = b * 4 + a
    local = [
        pltpu.make_async_copy(I.in_weight.at[pl.ds(0, 2)], S.wg.at[pl.ds(2 * b, 2)], sem_s["local"].at[0]),
        pltpu.make_async_copy(I.out_weight, S.ow.at[pl.ds(2 * own, 2)], sem_s["local"].at[1]),
        pltpu.make_async_copy(I.gate_weight, S.gw, sem_s["local"].at[2]),
        pltpu.make_async_copy(I.up_weight, S.uw, sem_s["local"].at[3]),
        pltpu.make_async_copy(I.down_weight, S.dw, sem_s["local"].at[4]),
        pltpu.make_async_copy(I.in_weight.at[pl.ds(2, 2)], S.wg.at[pl.ds(8 + 2 * b, 2)], sem_s["local"].at[5]),
    ]
    for copy in local:
        copy.start()

    pl.semaphore_wait(barrier, 30)
    local[0].wait()
    win0 = RingGather(S.wg, lambda p: 2 * p, 1, b, dev_b, sem_s["win0"], sem_r["win0"])
    win1 = RingGather(S.wg, lambda p: 8 + 2 * p, 1, b, dev_b, sem_s["win1"], sem_r["win1"])
    win0.start()

    gain = I.norm_gain[...]

    @pl.loop(0, T // 16)
    def _(i):
        rows = pl.ds(pl.multiple_of(i * 16, 16), 16)
        v = I.tokens[rows, :].astype(F32)
        inverse = lax.rsqrt(jnp.mean(v * v, axis=-1, keepdims=True) + EPSILON)
        normed = (v * inverse * gain).astype(BF16)
        for j in range(16):
            k = (1 - c) * (j % 4) + c * (j // 4)
            q = (1 - c) * (j // 4) + c * (j % 4)
            S.normed[4 * k + q, rows, :] = normed[:, j * FD : (j + 1) * FD]

    a_right, a_left, a_opp = mod(a + 1, 4), mod(a + 3, 4), mod(a + 2, 4)

    def tok_copy(src, dst, k, to):
        return rcopy(src, dst, sem_s["tok"].at[k], sem_r["tok"].at[k], dev_a(to))

    finish_later(tok_copy(S.normed.at[pl.ds(4 * a_opp, 2)], S.trelay.at[0], 0, a_right))
    finish_later(tok_copy(S.normed.at[pl.ds(4 * a_opp + 2, 2)], S.trelay.at[1], 1, a_left))
    finish_later(tok_copy(S.normed.at[pl.ds(4 * a_right, 4)], S.tok_g.at[pl.ds(4 * a, 4)], 2, a_right))
    finish_later(tok_copy(S.normed.at[pl.ds(4 * a_left, 4)], S.tok_g.at[pl.ds(4 * a, 4)], 3, a_left))
    tok_copy(S.trelay.at[0], S.trelay.at[0], 0, a_right).wait_recv()
    finish_later(tok_copy(S.trelay.at[0], S.tok_g.at[pl.ds(4 * a_left, 2)], 4, a_right))
    tok_copy(S.trelay.at[1], S.trelay.at[1], 1, a_left).wait_recv()
    finish_later(tok_copy(S.trelay.at[1], S.tok_g.at[pl.ds(4 * a_right + 2, 2)], 5, a_left))
    win0.forward()
    win0.sides()
    win0.opposite()
    for block, k in (
        (S.tok_g.at[pl.ds(4 * a_left, 4)], 2), (S.tok_g.at[pl.ds(4 * a_right, 4)], 3),
        (S.tok_g.at[pl.ds(4 * a_opp, 2)], 4), (S.tok_g.at[pl.ds(4 * a_opp + 2, 2)], 5),
    ):
        tok_copy(block, block, k, a_right).wait_recv()

    local[5].wait()
    win1.start()
    local[1].wait()
    ow1 = RingGather(S.ow, lambda p: (b * 4 + p) * 2, 1, a, dev_a, sem_s["ow1"], sem_r["ow1"])
    ow1.start()

    def project(branch, part, k, source):
        @pl.loop(0, C // 256)
        def _(n):
            cols = pl.ds(pl.multiple_of(n * 256, 256), 256)
            total = jnp.zeros((T, 256), F32)
            for q in range(4):
                at = 8 * branch + 2 * q
                weight = S.wg[at : at + 2, :, cols].reshape(FD, 256)
                total = total + jnp.dot(source[4 * k + q], weight, preferred_element_type=F32)
            part[pl.ds(2 * k, 2), :, cols] = total.reshape(2, T // 2, 256).astype(BF16)

    def project_all(branch, part, ring):
        project(branch, part, a_opp, S.tok_g)
        ring.start()
        project(branch, part, a_right, S.tok_g)
        project(branch, part, a_left, S.tok_g)
        ring.start_sides()
        project(branch, part, a, S.normed)

    mix = RingReduce(
        S.part_0, lambda p: 2 * p, 1, a, dev_a, S.m1_0, S.m2_0, S.ms_0, sem_s["mix"], sem_r["mix"]
    )
    gat = RingReduce(
        S.part_1, lambda p: 2 * p, 1, a, dev_a, S.m1_1, S.m2_1, S.ms_1, sem_s["gat"], sem_r["gat"]
    )
    project_all(0, S.part_0, mix)
    mix.middle()
    win1.forward()
    ow1.forward()

    def to_mixer(i, value):
        S.padf[pl.ds(pl.multiple_of(16 + i * (T // 2), 16), T // 2), :] = value.astype(F32)

    mix.finish(to_mixer)

    S.hsrc[...] = S.padf[T : T + 16, :].astype(BF16)
    finish_later(
        rcopy(S.hsrc, S.hdst, sem_s["halo"].at[0], sem_r["halo"].at[0], dev_s(mod(s + 1, 16)))
    )
    rcopy(S.hdst, S.hdst, sem_s["halo"].at[0], sem_r["halo"].at[0], dev_s(mod(s + 1, 16))).wait_recv()
    first = jnp.zeros((16, C), jnp.int32) + s
    S.padf[0:16, :] = jnp.where(first > 0, S.hdst[...].astype(F32), 0.0)

    @pl.loop(0, T // 16)
    def _(i):
        window = S.padf[pl.ds(pl.multiple_of(i * 16, 16), 32), :]
        total = I.conv_bias[...] + jnp.zeros((16, C), F32)
        for tap in range(4):
            total = total + I.conv_weight[tap : tap + 1, :] * window[13 + tap : 29 + tap, :]
        S.act[pl.ds(pl.multiple_of(i * 16, 16), 16), :] = silu(total).astype(BF16)

    def in_three(v):
        high = v.astype(BF16)
        rest = v - high.astype(F32)
        middle = rest.astype(BF16)
        return high, middle, (rest - middle.astype(F32)).astype(BF16)

    full = dot_t(S.act[...], I.proj_weight[...])
    S.feat[:, :, RANK:] = jnp.zeros((16, 8, 128), BF16)
    S.feat[:, :, :RANK] = full[:, :RANK].reshape(16, 8, RANK).astype(BF16)
    for k, term in enumerate(in_three(full[:, RANK:].reshape(16, 8, 2 * N))):
        S.feat[:, :, RANK + 32 * k : RANK + 32 * k + 32] = term
    for d in FAR_16:
        to = mod(e + d, 16)
        finish_later(rcopy(S.feat.at[to], S.frecv.at[e], sem_s["f1"].at[d], sem_r["f1"].at[d], (x, y, to)))
    ow1.sides()
    ow1.opposite()
    ow2 = RingGather(S.ow, lambda p: p * 8, 4, b, dev_b, sem_s["ow2"], sem_r["ow2"])
    ow2.start()
    win1.sides()
    win1.opposite()
    project_all(1, S.part_1, gat)
    S.frecv[e] = S.feat[e]
    for d in range(1, 16):
        block = S.frecv.at[mod(e + 16 - d, 16)]
        rcopy(block, block, sem_s["f1"].at[d], sem_r["f1"].at[d], (x, y, mod(e + 1, 16))).wait_recv()
    total = S.frecv[0].astype(F32)
    for d in range(1, 16):
        total = total + S.frecv[d].astype(F32)
    maps = total[:, RANK : RANK + 32] + total[:, RANK + 32 : RANK + 64] + total[:, RANK + 64 : RANK + 96]
    S.fsum[:, :RANK] = total[:, :RANK].astype(BF16)
    S.fsum[:, RANK:] = jnp.zeros((8, 128), BF16)
    for k, term in enumerate(in_three(maps)):
        S.fsum[:, RANK + 32 * k : RANK + 32 * k + 32] = term
    for d in FAR_16:
        to = mod(e + d, 16)
        finish_later(rcopy(S.fsum, S.fall.at[e], sem_s["f2"].at[d], sem_r["f2"].at[d], (x, y, to)))
    S.fall[e] = S.fsum[...]
    gat.middle()

    def to_gate(i, value):
        S.gate[pl.ds(pl.multiple_of(i * (T // 2), 16), T // 2), :] = value.astype(F32)

    gat.finish(to_gate)
    for d in range(1, 16):
        block = S.fall.at[mod(e + 16 - d, 16)]
        rcopy(block, block, sem_s["f2"].at[d], sem_r["f2"].at[d], (x, y, mod(e + 1, 16))).wait_recv()
    low = S.fall[:, :, :RANK].astype(F32).reshape(T, RANK).astype(BF16)
    upright_maps = jnp.transpose(S.fall[:, :, RANK:].astype(F32).reshape(T, 128))
    S.maps_t[...] = upright_maps[0:32, :] + upright_maps[32:64, :] + upright_maps[64:96, :]
    raw = jnp.dot(low, I.step_weight[...], preferred_element_type=F32) + I.step_bias[...]
    S.step[...] = jnp.maximum(raw, 0.0) + jnp.log1p(jnp.exp(-jnp.abs(raw)))
    S.drive[...] = S.step[...] * S.act[...].astype(F32)

    rate = -jnp.exp(I.decay_log[...])

    def scan(start, emit):
        def block(i, state):
            rows = pl.ds(pl.multiple_of(i * 8, 8), 8)
            steps, drives = S.step[rows, :], S.drive[rows, :]
            maps = pltpu.roll(S.maps_t[...], mod(T - 8 * i, T), 1)
            lines = []
            for t in range(8):
                state = jnp.exp(steps[t : t + 1, :] * rate) * state + drives[t : t + 1, :] * maps[:N, t : t + 1]
                if emit:
                    lines.append(jnp.sum(state * maps[N:, t : t + 1], axis=0, keepdims=True))
            if emit:
                S.y[rows, :] = jnp.concatenate(lines, axis=0)
            return state

        return lax.fori_loop(0, T // 8, block, start)

    zero_state = jnp.zeros((N, C), F32)
    S.stx[0:N, :] = scan(zero_state, False)
    S.stx[N : N + 8, :] = jnp.broadcast_to(jnp.sum(S.step[...], axis=0, keepdims=True), (8, C))

    def state_copy(d):
        return rcopy(
            S.stx, S.stall.at[s], sem_s["st"].at[d], sem_r["st"].at[d], dev_s(mod(s + d, 16))
        )

    for d in range(15, 0, -1):

        @pl.when(s + d < 16)
        def _():
            state_copy(d).start()

    ow2.forward()
    for d in range(1, 16):

        @pl.when(s - d >= 0)
        def _():
            block = S.stall.at[mod(s + 16 - d, 16)]
            rcopy(block, block, sem_s["st"].at[d], sem_r["st"].at[d], dev_s(mod(s + d, 16))).wait_recv()

    def compose(k, state):
        return jnp.exp(rate * S.stall[k, N : N + 1, :]) * state + S.stall[k, 0:N, :]

    scan(lax.fori_loop(0, s, compose, zero_state), True)

    @pl.loop(0, T // 16)
    def _(i):
        rows = pl.ds(pl.multiple_of(i * 16, 16), 16)
        scanned = S.y[rows, :] + I.skip_gain[...] * S.act[rows, :].astype(F32)
        S.gated[rows, :] = (scanned * silu(S.gate[rows, :])).astype(BF16)

    ow2.sides()
    ow2.opposite()

    @pl.loop(0, 16)
    def _(u):
        column = shard_of(mod(u, 4), u // 4)
        weight = S.ow[pl.ds(2 * u, 2)].reshape(C, FD)
        total = jnp.dot(S.gated[...], weight, preferred_element_type=F32).reshape(8, 2, 8, FD)
        cols = pl.ds(pl.multiple_of(column * FD, FD), FD)
        S.outp[0:8, :, cols] = total[:, 0].astype(BF16)
        S.outp[8:16, :, cols] = total[:, 1].astype(BF16)

    other = e + 1 - 2 * c
    pair = rcopy(S.outp.at[pl.ds(8 * (1 - c), 8)], S.pair, sem_s["pair"].at[0], sem_r["pair"].at[0], (x, y, other))
    finish_later(pair)
    pair.wait_recv()
    for d in FAR_8:
        zz = mod(z + d, 8)
        S.zs[zz] = (S.outp[8 * c + zz].astype(F32) + S.pair[zz].astype(F32)).astype(BF16)
        finish_later(
            rcopy(S.zs.at[zz], S.zrecv.at[z], sem_s["z"].at[d], sem_r["z"].at[d], (x, y, 2 * zz + c))
        )
    total = S.outp[8 * c + z].astype(F32) + S.pair[z].astype(F32)
    for d in range(1, 8):
        block = S.zrecv.at[mod(z + 8 - d, 8)]
        rcopy(block, block, sem_s["z"].at[d], sem_r["z"].at[d], (x, y, other)).wait_recv()
    for d in range(1, 8):
        total = total + S.zrecv[mod(z + d, 8)].astype(F32)

    both = I.tokens[pl.ds(pl.multiple_of(16 * z, 16), 16), :].astype(F32)
    core = jnp.zeros((8, D), jnp.int32) + c
    mine = jnp.where(core == 0, both[:8, :], both[8:, :])
    hid = (mine + total).astype(BF16).astype(F32)
    S.hid[...] = hid
    inverse = lax.rsqrt(jnp.mean(hid * hid, axis=-1, keepdims=True) + EPSILON)
    moe_in = (hid * inverse * I.moe_gain[...]).astype(BF16).astype(F32)
    twice = jnp.concatenate([moe_in, moe_in], axis=0).astype(BF16)
    logits = dot_t(twice, I.router_weight[...])[:8, :]

    ids = lax.broadcasted_iota(jnp.int32, (8, 16), 1)
    line_a, line_b = I.routes[0:1, :], I.routes[1:2, :]
    diagonal = lax.broadcasted_iota(jnp.int32, (8, 8), 0) == lax.broadcasted_iota(jnp.int32, (8, 8), 1)

    def upright(line):
        lines = jnp.where(diagonal, line.astype(F32), 0.0)
        return jnp.sum(lines, axis=1, keepdims=True).astype(jnp.int32)

    route_a, route_b = upright(line_a), upright(line_b)
    picked_a = jnp.sum(jnp.where(route_a == ids, logits, 0.0), axis=1, keepdims=True)
    picked_b = jnp.sum(jnp.where(route_b == ids, logits, 0.0), axis=1, keepdims=True)
    share_a = 1.0 / (1.0 + jnp.exp(picked_b - picked_a))
    share_b = 1.0 - share_a

    def chosen(slot, token, ra, rb, row_of):
        expert, slot_no = slot // 2, mod(slot, 2)
        match_a = jnp.where(ra == expert, 1.0, 0.0)
        match_b = jnp.where(rb == expert, 1.0, 0.0)
        named = match_a + match_b
        before = jnp.zeros_like(named)
        for t in range(7):
            before = before + jnp.where(token > t, row_of(named, t), 0.0)
        hit = jnp.where(before == slot_no.astype(F32), named, 0.0)
        return hit, match_a, match_b

    hit, match_a, match_b = chosen(
        lax.broadcasted_iota(jnp.int32, (8, ROWS), 1), lax.broadcasted_iota(jnp.int32, (8, ROWS), 0),
        route_a, route_b, lambda v, t: v[t : t + 1, :],
    )
    S.wt[...] = hit * (match_a * share_a + match_b * share_b)
    hit_t, _, _ = chosen(
        lax.broadcasted_iota(jnp.int32, (ROWS, 8), 0), lax.broadcasted_iota(jnp.int32, (ROWS, 8), 1),
        line_a, line_b, lambda v, t: v[:, t : t + 1],
    )
    for n in range(D // 512):
        cols = slice(n * 512, n * 512 + 512)
        slotted = jnp.zeros((ROWS, 512), F32)
        for t in range(8):
            slotted = slotted + hit_t[:, t : t + 1] * moe_in[t : t + 1, cols]
        S.slots[:, cols] = slotted
    for i in range(16):
        S.out3[i] = S.slots[2 * i : 2 * i + 2, :].astype(BF16)

    for d in FAR_16:
        to = mod(e + d, 16)
        finish_later(rcopy(S.out3.at[to], S.in3.at[e], sem_s["disp"].at[d], sem_r["disp"].at[d], (x, y, to)))
    S.in3[e] = S.out3[e]
    for d in range(1, 16):
        block = S.in3.at[mod(e + 16 - d, 16)]
        rcopy(block, block, sem_s["disp"].at[d], sem_r["disp"].at[d], (x, y, mod(e + 1, 16))).wait_recv()
    for i in range(16):
        S.slots[2 * i : 2 * i + 2, :] = S.in3[i].astype(F32)
    for h in range(2):
        S.rows[2 * own + h] = S.slots[16 * h : 16 * h + 16, :].astype(BF16)
    ag1 = RingGather(S.rows, lambda p: (b * 4 + p) * 2, 1, a, dev_a, sem_s["ag1"], sem_r["ag1"])
    ag2 = [
        RingGather(
            S.rows, lambda p, k=k: (p * 4 + k) * 2, 1, b, dev_b, sem_s["ag2"], sem_r["ag2"], 6 * i
        )
        for i, k in enumerate((a, a_left, a_right, a_opp))
    ]
    ag1.start()
    ag2[0].start()
    ag1.forward()
    ag2[0].forward()
    ag1.sides()
    ag2[1].start()
    ag2[2].start()
    ag1.opposite()
    ag2[3].start()
    for copy in local[2:5]:
        copy.wait()

    def hidden_units(bundles):
        count = len(bundles)
        tall = slice(0, count * T)
        S.acc_g[tall, :] = jnp.zeros((count * T, HU), F32)
        S.acc_u[tall, :] = jnp.zeros((count * T, HU), F32)

        @pl.loop(0, D // 1024)
        def _(n):
            cols = pl.ds(pl.multiple_of(n * 1024, 1024), 1024)
            rows = [S.rows[pl.ds(8 * p, 8), :, cols].reshape(T, 1024) for p in bundles]
            rows = rows[0] if count == 1 else jnp.concatenate(rows, axis=0)
            S.acc_g[tall, :] += dot_t(rows, S.gw[:, cols])
            S.acc_u[tall, :] += dot_t(rows, S.uw[:, cols])

        S.hidden[tall, :] = (silu(S.acc_g[tall, :]) * S.acc_u[tall, :]).astype(BF16)

    def down(bundles, chunk, target):
        tall = slice(0, len(bundles) * T)

        @pl.loop(0, WIDE // 512)
        def _(n):
            cols = pl.ds(pl.multiple_of(n * 512, 512), 512)
            wide = pl.ds(pl.multiple_of(chunk * WIDE + n * 512, 512), 512)
            result = jnp.dot(S.hidden[tall, :], S.dw[:, wide], preferred_element_type=F32)
            for k, p in enumerate(bundles):
                block = result[k * T : k * T + T].reshape(8, 16, 512)
                target[pl.ds(8 * p, 8), :, cols] = block.astype(BF16)

    parts = [getattr(S, f"y_{i}") for i in range(CHUNKS)]
    red1 = [
        RingReduce(
            parts[i], lambda p: p * 8, 4, b, dev_b, getattr(S, f"r1_{i}"), getattr(S, f"r2_{i}"),
            getattr(S, f"sm_{i}"), sem_s[f"red1_{i}"], sem_r[f"red1_{i}"],
        )
        for i in range(CHUNKS)
    ]
    red2 = [
        RingReduce(
            getattr(S, f"zin_{i}"), lambda p: p * 2, 1, a, dev_a, getattr(S, f"q1_{i}"), getattr(S, f"q2_{i}"),
            getattr(S, f"qm_{i}"), sem_s[f"red2_{i}"], sem_r[f"red2_{i}"],
        )
        for i in range(CHUNKS)
    ]
    b_right, b_left, b_opp = red1[0].right, red1[0].left, red1[0].opp

    hidden_units([b])
    for i in range(CHUNKS):
        down([b], i, parts[i])
    for ring in ag2[1:]:
        ring.forward()
    for ring in ag2:
        ring.sides()
    hidden_units([b_left, b_right])
    for i in range(CHUNKS):
        down([b_left, b_right], i, parts[i])
        red1[i].start_sides()
    for ring in ag2:
        ring.opposite()
    hidden_units([b_opp])

    for i in range(CHUNKS):
        down([b_opp], i, parts[i])
        red1[i].start()

    def to_second(i):
        def store(k, value):
            getattr(S, f"zin_{i}")[k] = value

        return store

    def to_slots(i):
        def store(k, value):
            S.slots[pl.ds(pl.multiple_of(16 * k, 16), 16), i * WIDE : (i + 1) * WIDE] = value.astype(F32)

        return store

    def send_back(h):
        ret, back = getattr(S, f"ret_{h}"), getattr(S, f"back_{h}")
        half = slice(h * (D // 2), (h + 1) * (D // 2))
        for i in range(16):
            ret[i] = S.slots[2 * i : 2 * i + 2, half].astype(BF16)
        for d in FAR_16:
            to = mod(e + d, 16)
            finish_later(
                rcopy(ret.at[to], back.at[e], sem_s[f"ret_{h}"].at[d], sem_r[f"ret_{h}"].at[d], (x, y, to))
            )
        back[e] = ret[e]

    for i in range(CHUNKS):
        red1[i].middle()
    for i in range(CHUNKS):
        red1[i].finish(to_second(i))
        red2[i].start()
        red2[i].start_sides()
        if i >= 1:
            red2[i - 1].middle()
        if i >= 2:
            red2[i - 2].finish(to_slots(i - 2))
    send_back(0)
    red2[CHUNKS - 1].middle()
    red2[CHUNKS - 2].finish(to_slots(CHUNKS - 2))
    red2[CHUNKS - 1].finish(to_slots(CHUNKS - 1))
    send_back(1)
    for h in range(2):
        for d in range(1, 16):
            block = getattr(S, f"back_{h}").at[mod(e + 16 - d, 16)]
            rcopy(
                block, block, sem_s[f"ret_{h}"].at[d], sem_r[f"ret_{h}"].at[d], (x, y, mod(e + 1, 16))
            ).wait_recv()

    weights = S.wt[...]
    for h in range(2):
        half = slice(h * (D // 2), (h + 1) * (D // 2))
        mixed = S.hid[:, half]
        for i in range(16):
            pair_rows = getattr(S, f"back_{h}")[i].astype(F32)
            for m in range(2):
                j = 2 * i + m
                mixed = mixed + weights[:, j : j + 1] * pair_rows[m : m + 1, :]
        out_ref[:, half] = mixed.astype(BF16)

    for copy in drains:
        copy.wait_send()
    for ring in (win0, win1, mix, gat, ow1, ow2, ag1, *ag2, *red1, *red2):
        ring.drain()
    for d in range(1, 16):

        @pl.when(s + d < 16)
        def _():
            state_copy(d).wait_send()


def local_step(
    tokens, norm_gain, in_weight, conv_weight, conv_bias, proj_weight, step_weight, step_bias, decay_log,
    skip_gain, out_weight, moe_gain, router_weight, routes, gate_weight, up_weight, down_weight,
):
    operands = (
        tokens, norm_gain[None], jnp.swapaxes(in_weight, 0, 1).reshape(4, FD // 2, C), conv_weight, conv_bias[None],
        jnp.transpose(proj_weight), step_weight, step_bias[None], jnp.transpose(decay_log), skip_gain[None],
        out_weight.reshape(2, C // 2, FD), moe_gain[None], jnp.transpose(router_weight), jnp.transpose(routes),
        jnp.transpose(gate_weight[0]), jnp.transpose(up_weight[0]), down_weight[0],
    )
    spaces = {"v": pltpu.VMEM, "a": pl.ANY}
    return pl.pallas_call(
        kernel,
        out_shape=jax.ShapeDtypeStruct((8, D), BF16),
        in_specs=[pl.BlockSpec(memory_space=spaces[kind]) for _, kind in INPUTS],
        out_specs=pl.BlockSpec(memory_space=pltpu.VMEM),
        scratch_shapes=[pltpu.VMEM(shape, dtype) for shape, dtype in SCRATCH.values()]
        + [pltpu.SemaphoreType.DMA((count,)) for count in SEMS.values()] * 2,
        compiler_params=pltpu.CompilerParams(
            collective_id=0, has_side_effects=True, vmem_limit_bytes=60 * 1024 * 1024
        ),
    )(*operands)


def solution(mesh):
    split = Mesh(mesh.devices.reshape(4, 4, mesh.shape["expert"]), ("seq_0", "seq_1", "expert"))
    in_specs = (
        P(SEQ, None),
        P(),
        P(SEQ, None, "expert"),
        P(None, "expert"),
        P("expert"),
        P("expert", None),
        P(None, "expert"),
        P("expert"),
        P("expert", None),
        P("expert"),
        P("expert", SEQ),
        P(),
        P(),
        P(SEQ_EXPERT, None),
        P("expert", None, SEQ),
        P("expert", None, SEQ),
        P("expert", SEQ, None),
    )
    out_specs = P(SEQ_EXPERT, None)
    return jax.shard_map(local_step, mesh=split, in_specs=in_specs, out_specs=out_specs, check_vma=False)
```

```python
import types

import jax
import jax.numpy as jnp
from jax import lax
from jax.experimental import pallas as pl
from jax.experimental.pallas import tpu as pltpu
from jax.sharding import Mesh
from jax.sharding import PartitionSpec as P

SEQ = ("seq_0", "seq_1")
SEQ_EXPERT = ("seq_0", "seq_1", "expert")
EPSILON = 1e-06
F32 = jnp.float32
BF16 = jnp.bfloat16

D = 4096
T = 128
C = 512
FD = 256
N = 16
RANK = 256
HU = 448
ROWS = 32


def mod(v, n):
    return lax.rem(v, n)


def rcopy(src, dst, send, recv, device):
    return pltpu.make_async_remote_copy(
        src_ref=src,
        dst_ref=dst,
        send_sem=send,
        recv_sem=recv,
        device_id=device,
        device_id_type=pl.DeviceIdType.MESH,
    )


def dot_t(left, right):
    return lax.dot_general(left, right, (((1,), (1,)), ((), ())), preferred_element_type=F32)


def silu(v):
    return v / (1.0 + jnp.exp(-v))


class RingGather:
    def __init__(self, buf, base, half, pos, dev, send, recv, offset=0):
        self.buf, self.base, self.half, self.dev = buf, base, half, dev
        self.send, self.recv, self.offset = send, recv, offset
        self.pos, self.right, self.left, self.opp = pos, mod(pos + 1, 4), mod(pos + 3, 4), mod(pos + 2, 4)
        self.started = []

    def part(self, pos, h):
        return self.buf.at[pl.ds(self.base(pos) + h * self.half, self.half)]

    def go(self, pos, h, to, k):
        block = self.part(pos, h)
        k = k + self.offset
        copy = rcopy(block, block, self.send.at[k], self.recv.at[k], self.dev(to))
        copy.start()
        self.started.append(copy)

    def arrived(self, pos, h, k):
        block = self.part(pos, h)
        k = k + self.offset
        rcopy(block, block, self.send.at[k], self.recv.at[k], self.dev(self.right)).wait_recv()

    def start(self):
        self.go(self.pos, 0, self.right, 0)
        self.go(self.pos, 1, self.left, 3)
        self.go(self.pos, 1, self.right, 1)
        self.go(self.pos, 0, self.left, 2)

    def forward(self):
        self.arrived(self.left, 0, 0)
        self.go(self.left, 0, self.right, 4)
        self.arrived(self.right, 1, 3)
        self.go(self.right, 1, self.left, 5)

    def sides(self):
        self.arrived(self.left, 1, 1)
        self.arrived(self.right, 0, 2)

    def opposite(self):
        self.arrived(self.opp, 0, 4)
        self.arrived(self.opp, 1, 5)

    def drain(self):
        for copy in self.started:
            copy.wait_send()


class RingReduce:
    def __init__(self, part, base, half, pos, dev, first, second, summed, send, recv):
        self.buf, self.base, self.half, self.dev = part, base, half, dev
        self.first, self.second, self.summed = first, second, summed
        self.send, self.recv = send, recv
        self.pos, self.right, self.left, self.opp = pos, mod(pos + 1, 4), mod(pos + 3, 4), mod(pos + 2, 4)
        self.started = []

    def part(self, pos, h):
        return self.buf.at[pl.ds(self.base(pos) + h * self.half, self.half)]

    def go(self, src, dst, to, k):
        copy = rcopy(src, dst, self.send.at[k], self.recv.at[k], self.dev(to))
        copy.start()
        self.started.append(copy)

    def arrived(self, dst, k):
        rcopy(dst, dst, self.send.at[k], self.recv.at[k], self.dev(self.right)).wait_recv()

    def start(self):
        self.go(self.part(self.opp, 0), self.first.at[0], self.right, 0)
        self.go(self.part(self.opp, 1), self.first.at[1], self.left, 1)

    def start_sides(self):
        h = self.half
        self.go(self.part(self.right, 1), self.second.at[0, pl.ds(h, h)], self.right, 2)
        self.go(self.part(self.left, 0), self.second.at[1, pl.ds(0, h)], self.left, 3)

    def middle(self):
        h = self.half
        for side, (owner, which) in enumerate(((self.right, 0), (self.left, 1))):
            self.arrived(self.first.at[side], side)
            at = self.base(owner) + which * h

            @pl.loop(0, h)
            def _(i):
                total = self.buf[at + i].astype(F32) + self.first[side, i].astype(F32)
                self.summed[side, i] = total.astype(BF16)

            self.go(self.summed.at[side], self.second.at[side, pl.ds(which * h, h)], owner, 4 + side)

    def finish(self, store):
        h = self.half
        self.arrived(self.second.at[0, pl.ds(h, h)], 2)
        self.arrived(self.second.at[1, pl.ds(0, h)], 3)
        self.arrived(self.second.at[0, pl.ds(0, h)], 4)
        self.arrived(self.second.at[1, pl.ds(h, h)], 5)
        at = self.base(self.pos)

        @pl.loop(0, 2 * h)
        def _(i):
            total = self.buf[at + i].astype(F32) + self.second[0, i].astype(F32)
            store(i, (total + self.second[1, i].astype(F32)).astype(BF16))

    def drain(self):
        for copy in self.started:
            copy.wait_send()


INPUTS = (
    ("tokens", "v"), ("norm_gain", "v"), ("in_weight", "a"), ("conv_weight", "v"), ("conv_bias", "v"),
    ("proj_weight", "v"), ("step_weight", "v"), ("step_bias", "v"), ("decay_log", "v"), ("skip_gain", "v"),
    ("out_weight", "a"), ("moe_gain", "v"), ("router_weight", "v"), ("routes", "v"),
    ("gate_weight", "a"), ("up_weight", "a"), ("down_weight", "a"),
)

CHUNKS = 4
WIDE = D // CHUNKS

SCRATCH = {
    "normed": ((16, T, FD), BF16),
    "tok_g": ((16, T, FD), BF16),
    "trelay": ((2, 2, T, FD), BF16),
    "wraw": ((FD, 2, C), BF16),
    "wg": ((16, FD // 2, C), BF16),
    "part_0": ((8, T // 2, C), BF16),
    "part_1": ((8, T // 2, C), BF16),
    "m1_0": ((2, 1, T // 2, C), BF16),
    "m2_0": ((2, 2, T // 2, C), BF16),
    "ms_0": ((2, 1, T // 2, C), BF16),
    "m1_1": ((2, 1, T // 2, C), BF16),
    "m2_1": ((2, 2, T // 2, C), BF16),
    "ms_1": ((2, 1, T // 2, C), BF16),
    "padf": ((T + 16, C), F32),
    "gate": ((T, C), F32),
    "hsrc": ((16, C), BF16),
    "hdst": ((16, C), BF16),
    "act": ((T, C), BF16),
    "feat": ((16, 8, 384), BF16),
    "frecv": ((16, 8, 384), BF16),
    "fsum": ((8, 384), BF16),
    "fall": ((16, 8, 384), BF16),
    "step": ((T, C), F32),
    "drive": ((T, C), F32),
    "maps_t": ((ROWS, T), F32),
    "y": ((T, C), F32),
    "stx": ((N, C), BF16),
    "stall": ((16, N, C), BF16),
    "sumx": ((8, C), F32),
    "sumall": ((16, 8, C), F32),
    "passed": ((16, N, C), F32),
    "gated": ((T, C), BF16),
    "ow": ((32, C // 2, FD), BF16),
    "outp": ((16, 8, D), BF16),
    "pair": ((8, 8, D), BF16),
    "zs": ((8, 8, D), BF16),
    "zrecv": ((8, 8, D), BF16),
    "zs4": ((2, 8, D // 2), BF16),
    "z4r": ((2, 8, D // 2), BF16),
    "hid": ((8, D), F32),
    "wt": ((8, ROWS), F32),
    "slots": ((ROWS, D), F32),
    "out3": ((16, 2, D), BF16),
    "in3": ((16, 2, D), BF16),
    "rows": ((32, 16, D), BF16),
    "gw": ((HU, D), BF16),
    "uw": ((HU, D), BF16),
    "dw": ((HU, D), BF16),
    "acc_g": ((2 * T, HU), F32),
    "acc_u": ((2 * T, HU), F32),
    "hidden": ((2 * T, HU), BF16),
    **{
        f"{name}_{chunk}": ((*shape, 16, WIDE), BF16)
        for chunk in range(CHUNKS)
        for name, shape in {
            "y": (32,), "r1": (2, 4), "r2": (2, 8), "sm": (2, 4), "zin": (8,), "q1": (2, 1), "q2": (2, 2), "qm": (2, 1),
        }.items()
    },
    "ret_0": ((16, 2, D // 2), BF16),
    "ret_1": ((16, 2, D // 2), BF16),
    "back_0": ((16, 2, D // 2), BF16),
    "back_1": ((16, 2, D // 2), BF16),
}

SEMS = {
    "local": 6,
    "tok": 6, "win0": 6, "win1": 6, "mix": 6, "gat": 6, "halo": 1, "f1": 16, "f2": 16, "st": 16, "sum": 16, "ow1": 6, "ow2": 6,
    "pair": 1, "z": 8, "z4": 2, "disp": 16, "ag1": 6, "ag2": 24,
    **{f"{name}_{chunk}": 6 for name in ("red1", "red2") for chunk in range(CHUNKS)},
    "ret_0": 16, "ret_1": 16,
}

FAR_16 = (8, 7, 9, 6, 10, 5, 11, 4, 12, 3, 13, 2, 14, 1, 15)


def kernel(*refs):
    count = len(INPUTS)
    I = types.SimpleNamespace(**{name: r for (name, _), r in zip(INPUTS, refs[:count])})
    out_ref = refs[count]
    rest = refs[count + 1 :]
    S = types.SimpleNamespace(**dict(zip(SCRATCH, rest[: len(SCRATCH)])))
    rest = rest[len(SCRATCH) :]
    sem_s = dict(zip(SEMS, rest[: len(SEMS)]))
    sem_r = dict(zip(SEMS, rest[len(SEMS) :]))

    x, y, e = lax.axis_index("seq_0"), lax.axis_index("seq_1"), lax.axis_index("expert")
    c, z = mod(e, 2), e // 2
    s = 4 * x + y
    a = c * x + (1 - c) * y
    b = (1 - c) * x + c * y

    def dev_a(k):
        return (x + c * (k - x), y + (1 - c) * (k - y), e)

    def dev_b(k):
        return (x + (1 - c) * (k - x), y + c * (k - y), e)

    def dev_s(k):
        return (k // 4, mod(k, 4), e)

    def shard_of(k, q):
        return c * (4 * k + q) + (1 - c) * (4 * q + k)

    drains = []

    def column_exchange(src, dst, name):
        send, recv = sem_s[name], sem_r[name]

        def piece(d):
            to = mod(e + d, 16)
            finish_later(rcopy(src.at[to], dst.at[e], send.at[d], recv.at[d], (x, y, to)))

        for d in FAR_16:
            piece(d)

    def finish_later(copy):
        copy.start()
        drains.append(copy)

    barrier = pltpu.get_barrier_semaphore()
    for d in range(1, 16):
        pl.semaphore_signal(barrier, inc=1, device_id=(x, y, mod(e + d, 16)), device_id_type=pl.DeviceIdType.MESH)
        pl.semaphore_signal(barrier, inc=1, device_id=dev_s(mod(s + d, 16)), device_id_type=pl.DeviceIdType.MESH)

    own = b * 4 + a
    local = [
        pltpu.make_async_copy(I.in_weight, S.wraw, sem_s["local"].at[0]),
        pltpu.make_async_copy(I.out_weight, S.ow.at[pl.ds(2 * own, 2)], sem_s["local"].at[1]),
        pltpu.make_async_copy(I.gate_weight, S.gw, sem_s["local"].at[2]),
        pltpu.make_async_copy(I.up_weight, S.uw, sem_s["local"].at[3]),
        pltpu.make_async_copy(I.down_weight, S.dw, sem_s["local"].at[4]),
    ]
    for copy in (local[0], local[1]):
        copy.start()

    gain = I.norm_gain[...]

    @pl.loop(0, T // 16)
    def _(i):
        rows = pl.ds(pl.multiple_of(i * 16, 16), 16)
        v = I.tokens[rows, :].astype(F32)
        inverse = lax.rsqrt(jnp.mean(v * v, axis=-1, keepdims=True) + EPSILON)
        normed = (v * inverse * gain).astype(BF16)
        for j in range(16):
            k = (1 - c) * (j % 4) + c * (j // 4)
            q = (1 - c) * (j // 4) + c * (j % 4)
            S.normed[4 * k + q, rows, :] = normed[:, j * FD : (j + 1) * FD]

    local[0].wait()
    for p in range(2):
        for h in range(2):
            S.wg[8 * p + 2 * b + h] = S.wraw[128 * h : 128 * h + 128, p, :]
    pl.semaphore_wait(barrier, 30)
    win0 = RingGather(S.wg, lambda p: 2 * p, 1, b, dev_b, sem_s["win0"], sem_r["win0"])
    win1 = RingGather(S.wg, lambda p: 8 + 2 * p, 1, b, dev_b, sem_s["win1"], sem_r["win1"])
    win0.start()

    a_right, a_left, a_opp = mod(a + 1, 4), mod(a + 3, 4), mod(a + 2, 4)

    def tok_copy(src, dst, k, to):
        return rcopy(src, dst, sem_s["tok"].at[k], sem_r["tok"].at[k], dev_a(to))

    finish_later(tok_copy(S.normed.at[pl.ds(4 * a_opp, 2)], S.trelay.at[0], 0, a_right))
    finish_later(tok_copy(S.normed.at[pl.ds(4 * a_opp + 2, 2)], S.trelay.at[1], 1, a_left))
    finish_later(tok_copy(S.normed.at[pl.ds(4 * a_right, 4)], S.tok_g.at[pl.ds(4 * a, 4)], 2, a_right))
    finish_later(tok_copy(S.normed.at[pl.ds(4 * a_left, 4)], S.tok_g.at[pl.ds(4 * a, 4)], 3, a_left))
    tok_copy(S.trelay.at[0], S.trelay.at[0], 0, a_right).wait_recv()
    finish_later(tok_copy(S.trelay.at[0], S.tok_g.at[pl.ds(4 * a_left, 2)], 4, a_right))
    tok_copy(S.trelay.at[1], S.trelay.at[1], 1, a_left).wait_recv()
    finish_later(tok_copy(S.trelay.at[1], S.tok_g.at[pl.ds(4 * a_right + 2, 2)], 5, a_left))
    win0.forward()
    win0.sides()
    win0.opposite()
    for block, k in (
        (S.tok_g.at[pl.ds(4 * a_left, 4)], 2), (S.tok_g.at[pl.ds(4 * a_right, 4)], 3),
        (S.tok_g.at[pl.ds(4 * a_opp, 2)], 4), (S.tok_g.at[pl.ds(4 * a_opp + 2, 2)], 5),
    ):
        tok_copy(block, block, k, a_right).wait_recv()

    win1.start()
    local[1].wait()
    ow1 = RingGather(S.ow, lambda p: (b * 4 + p) * 2, 1, a, dev_a, sem_s["ow1"], sem_r["ow1"])
    ow1.start()

    def project(branch, part, k, source):
        @pl.loop(0, C // 256)
        def _(n):
            cols = pl.ds(pl.multiple_of(n * 256, 256), 256)
            total = jnp.zeros((T, 256), F32)
            for q in range(4):
                at = 8 * branch + 2 * q
                weight = S.wg[at : at + 2, :, cols].reshape(FD, 256)
                total = total + jnp.dot(source[4 * k + q], weight, preferred_element_type=F32)
            part[pl.ds(2 * k, 2), :, cols] = total.reshape(2, T // 2, 256).astype(BF16)

    def project_all(branch, part, ring):
        project(branch, part, a_opp, S.tok_g)
        ring.start()
        project(branch, part, a_right, S.tok_g)
        project(branch, part, a_left, S.tok_g)
        ring.start_sides()
        project(branch, part, a, S.normed)

    mix = RingReduce(
        S.part_0, lambda p: 2 * p, 1, a, dev_a, S.m1_0, S.m2_0, S.ms_0, sem_s["mix"], sem_r["mix"]
    )
    gat = RingReduce(
        S.part_1, lambda p: 2 * p, 1, a, dev_a, S.m1_1, S.m2_1, S.ms_1, sem_s["gat"], sem_r["gat"]
    )
    project_all(0, S.part_0, mix)
    mix.middle()
    win1.forward()
    ow1.forward()

    def to_mixer(i, value):
        S.padf[pl.ds(pl.multiple_of(16 + i * (T // 2), 16), T // 2), :] = value.astype(F32)

    mix.finish(to_mixer)

    S.hsrc[...] = S.padf[T : T + 16, :].astype(BF16)
    finish_later(
        rcopy(S.hsrc, S.hdst, sem_s["halo"].at[0], sem_r["halo"].at[0], dev_s(mod(s + 1, 16)))
    )

    def convolve(i):
        window = S.padf[pl.ds(pl.multiple_of(i * 16, 16), 32), :]
        total = I.conv_bias[...] + jnp.zeros((16, C), F32)
        for tap in range(4):
            total = total + I.conv_weight[tap : tap + 1, :] * window[13 + tap : 29 + tap, :]
        S.act[pl.ds(pl.multiple_of(i * 16, 16), 16), :] = silu(total).astype(BF16)

    pl.loop(1, T // 16)(convolve)
    rcopy(S.hdst, S.hdst, sem_s["halo"].at[0], sem_r["halo"].at[0], dev_s(mod(s + 1, 16))).wait_recv()
    first = jnp.zeros((16, C), jnp.int32) + s
    S.padf[0:16, :] = jnp.where(first > 0, S.hdst[...].astype(F32), 0.0)
    convolve(0)

    def in_three(v):
        high = v.astype(BF16)
        rest = v - high.astype(F32)
        middle = rest.astype(BF16)
        return high, middle, (rest - middle.astype(F32)).astype(BF16)

    full = dot_t(S.act[...], I.proj_weight[...])
    S.feat[:, :, RANK:] = jnp.zeros((16, 8, 128), BF16)
    S.feat[:, :, :RANK] = full[:, :RANK].reshape(16, 8, RANK).astype(BF16)
    for k, term in enumerate(in_three(full[:, RANK:].reshape(16, 8, 2 * N))):
        S.feat[:, :, RANK + 32 * k : RANK + 32 * k + 32] = term
    for d in FAR_16:
        to = mod(e + d, 16)
        finish_later(rcopy(S.feat.at[to], S.frecv.at[e], sem_s["f1"].at[d], sem_r["f1"].at[d], (x, y, to)))
    ow1.sides()
    ow1.opposite()
    ow2 = RingGather(S.ow, lambda p: p * 8, 4, b, dev_b, sem_s["ow2"], sem_r["ow2"])
    ow2.start()
    win1.sides()
    win1.opposite()
    project_all(1, S.part_1, gat)
    S.frecv[e] = S.feat[e]
    for d in range(1, 16):
        block = S.frecv.at[mod(e + 16 - d, 16)]
        rcopy(block, block, sem_s["f1"].at[d], sem_r["f1"].at[d], (x, y, mod(e + 1, 16))).wait_recv()
    total = S.frecv[0].astype(F32)
    for d in range(1, 16):
        total = total + S.frecv[d].astype(F32)
    maps = total[:, RANK : RANK + 32] + total[:, RANK + 32 : RANK + 64] + total[:, RANK + 64 : RANK + 96]
    S.fsum[:, :RANK] = total[:, :RANK].astype(BF16)
    S.fsum[:, RANK:] = jnp.zeros((8, 128), BF16)
    for k, term in enumerate(in_three(maps)):
        S.fsum[:, RANK + 32 * k : RANK + 32 * k + 32] = term
    for d in FAR_16:
        to = mod(e + d, 16)
        finish_later(rcopy(S.fsum, S.fall.at[e], sem_s["f2"].at[d], sem_r["f2"].at[d], (x, y, to)))
    S.fall[e] = S.fsum[...]
    gat.middle()

    def to_gate(i, value):
        S.gate[pl.ds(pl.multiple_of(i * (T // 2), 16), T // 2), :] = value.astype(F32)

    gat.finish(to_gate)
    for d in range(1, 16):
        block = S.fall.at[mod(e + 16 - d, 16)]
        rcopy(block, block, sem_s["f2"].at[d], sem_r["f2"].at[d], (x, y, mod(e + 1, 16))).wait_recv()
    low = S.fall[:, :, :RANK].astype(F32).reshape(T, RANK).astype(BF16)
    upright_maps = jnp.transpose(S.fall[:, :, RANK:].astype(F32).reshape(T, 128))
    S.maps_t[...] = upright_maps[0:32, :] + upright_maps[32:64, :] + upright_maps[64:96, :]
    raw = jnp.dot(low, I.step_weight[...], preferred_element_type=F32) + I.step_bias[...]
    S.step[...] = jnp.maximum(raw, 0.0) + jnp.log1p(jnp.exp(-jnp.abs(raw)))
    S.drive[...] = S.step[...] * S.act[...].astype(F32)

    rate = -jnp.exp(I.decay_log[...])

    def scan(start, emit):
        def block(i, state):
            rows = pl.ds(pl.multiple_of(i * 8, 8), 8)
            steps, drives = S.step[rows, :], S.drive[rows, :]
            maps = pltpu.roll(S.maps_t[...], mod(T - 8 * i, T), 1)
            lines = []
            for t in range(8):
                state = jnp.exp(steps[t : t + 1, :] * rate) * state + drives[t : t + 1, :] * maps[:N, t : t + 1]
                if emit:
                    lines.append(jnp.sum(state * maps[N:, t : t + 1], axis=0, keepdims=True))
            if emit:
                S.y[rows, :] = jnp.concatenate(lines, axis=0)
            return state

        return lax.fori_loop(0, T // 8, block, start)

    def sum_copy(d):
        to = dev_s(mod(s + d, 16))
        return rcopy(S.sumx, S.sumall.at[s], sem_s["sum"].at[d], sem_r["sum"].at[d], to)

    def state_copy(d):
        to = dev_s(mod(s + d, 16))
        return rcopy(S.stx, S.stall.at[s], sem_s["st"].at[d], sem_r["st"].at[d], to)

    def to_later(copy_of):
        for d in range(15, 0, -1):

            @pl.when(s + d < 16)
            def _():
                copy_of(d).start()

    for copy in local[2:5]:
        copy.start()
    S.sumx[...] = jnp.broadcast_to(jnp.sum(S.step[...], axis=0, keepdims=True), (8, C))
    to_later(sum_copy)
    zero_state = jnp.zeros((N, C), F32)
    S.stx[...] = scan(zero_state, False).astype(BF16)
    to_later(state_copy)

    ow2.forward()
    for d in range(1, 16):

        @pl.when(s - d >= 0)
        def _():
            block = S.sumall.at[mod(s + 16 - d, 16)]
            rcopy(block, block, sem_s["sum"].at[d], sem_r["sum"].at[d], dev_s(mod(s + d, 16))).wait_recv()

    def passed(i, steps):
        k = s - 1 - i
        S.passed[k] = jnp.exp(rate * steps)
        return steps + S.sumall[k, 0:1, :]

    lax.fori_loop(0, s, passed, jnp.zeros((1, C), F32))
    for d in range(1, 16):

        @pl.when(s - d >= 0)
        def _():
            block = S.stall.at[mod(s + 16 - d, 16)]
            rcopy(block, block, sem_s["st"].at[d], sem_r["st"].at[d], dev_s(mod(s + d, 16))).wait_recv()

    def compose(k, state):
        return state + S.passed[k] * S.stall[k].astype(F32)

    scan(lax.fori_loop(0, s, compose, zero_state), True)

    @pl.loop(0, T // 16)
    def _(i):
        rows = pl.ds(pl.multiple_of(i * 16, 16), 16)
        scanned = S.y[rows, :] + I.skip_gain[...] * S.act[rows, :].astype(F32)
        S.gated[rows, :] = (scanned * silu(S.gate[rows, :])).astype(BF16)

    ow2.sides()
    ow2.opposite()

    @pl.loop(0, 16)
    def _(u):
        column = shard_of(mod(u, 4), u // 4)
        weight = S.ow[pl.ds(2 * u, 2)].reshape(C, FD)
        total = jnp.dot(S.gated[...], weight, preferred_element_type=F32).reshape(8, 2, 8, FD)
        cols = pl.ds(pl.multiple_of(column * FD, FD), FD)
        S.outp[0:8, :, cols] = total[:, 0].astype(BF16)
        S.outp[8:16, :, cols] = total[:, 1].astype(BF16)

    other = e + 1 - 2 * c
    pair = rcopy(S.outp.at[pl.ds(8 * (1 - c), 8)], S.pair, sem_s["pair"].at[0], sem_r["pair"].at[0], (x, y, other))
    finish_later(pair)
    pair.wait_recv()

    def chip_sum(zz):
        return S.outp[8 * c + zz].astype(F32) + S.pair[zz].astype(F32)

    def z_copy(d):
        zz = mod(z + d, 8)
        finish_later(
            rcopy(S.zs.at[zz], S.zrecv.at[z], sem_s["z"].at[d], sem_r["z"].at[d], (x, y, 2 * zz + c))
        )

    across = chip_sum(mod(z + 4, 8)).astype(BF16)
    for h, step in ((0, 2), (1, 14)):
        S.zs4[h] = across[:, h * (D // 2) : (h + 1) * (D // 2)]
        finish_later(
            rcopy(
                S.zs4.at[h], S.z4r.at[h], sem_s["z4"].at[h], sem_r["z4"].at[h], (x, y, mod(e + step, 16))
            )
        )
    for d in (2, 6, 1, 7):
        zz = mod(z + d, 8)
        S.zs[zz] = chip_sum(zz).astype(BF16)
        z_copy(d)
    for h, d in ((0, 3), (1, 5)):
        zz = mod(z + d, 8)
        plain = chip_sum(zz)
        rcopy(S.z4r.at[h], S.z4r.at[h], sem_s["z4"].at[h], sem_r["z4"].at[h], (x, y, other)).wait_recv()
        arrived = S.z4r[h].astype(F32)
        for k in range(2):
            half = slice(k * (D // 2), (k + 1) * (D // 2))
            S.zs[zz, :, half] = (plain[:, half] + arrived if k == h else plain[:, half]).astype(BF16)
        z_copy(d)
    total = chip_sum(z)
    for d in (1, 2, 3, 5, 6, 7):
        block = S.zrecv.at[mod(z + 8 - d, 8)]
        rcopy(block, block, sem_s["z"].at[d], sem_r["z"].at[d], (x, y, other)).wait_recv()
    for d in (1, 2, 3, 5, 6, 7):
        total = total + S.zrecv[mod(z + d, 8)].astype(F32)

    both = I.tokens[pl.ds(pl.multiple_of(16 * z, 16), 16), :].astype(F32)
    core = jnp.zeros((8, D), jnp.int32) + c
    mine = jnp.where(core == 0, both[:8, :], both[8:, :])
    hid = (mine + total).astype(BF16).astype(F32)
    S.hid[...] = hid
    inverse = lax.rsqrt(jnp.mean(hid * hid, axis=-1, keepdims=True) + EPSILON)
    moe_in = (hid * inverse * I.moe_gain[...]).astype(BF16).astype(F32)
    twice = jnp.concatenate([moe_in, moe_in], axis=0).astype(BF16)
    logits = dot_t(twice, I.router_weight[...])[:8, :]

    ids = lax.broadcasted_iota(jnp.int32, (8, 16), 1)
    line_a, line_b = I.routes[0:1, :], I.routes[1:2, :]
    diagonal = lax.broadcasted_iota(jnp.int32, (8, 8), 0) == lax.broadcasted_iota(jnp.int32, (8, 8), 1)

    def upright(line):
        lines = jnp.where(diagonal, line.astype(F32), 0.0)
        return jnp.sum(lines, axis=1, keepdims=True).astype(jnp.int32)

    route_a, route_b = upright(line_a), upright(line_b)
    picked_a = jnp.sum(jnp.where(route_a == ids, logits, 0.0), axis=1, keepdims=True)
    picked_b = jnp.sum(jnp.where(route_b == ids, logits, 0.0), axis=1, keepdims=True)
    share_a = 1.0 / (1.0 + jnp.exp(picked_b - picked_a))
    share_b = 1.0 - share_a

    def chosen(slot, token, ra, rb, row_of):
        expert, slot_no = slot // 2, mod(slot, 2)
        match_a = jnp.where(ra == expert, 1.0, 0.0)
        match_b = jnp.where(rb == expert, 1.0, 0.0)
        named = match_a + match_b
        before = jnp.zeros_like(named)
        for t in range(7):
            before = before + jnp.where(token > t, row_of(named, t), 0.0)
        hit = jnp.where(before == slot_no.astype(F32), named, 0.0)
        return hit, match_a, match_b

    hit, match_a, match_b = chosen(
        lax.broadcasted_iota(jnp.int32, (8, ROWS), 1), lax.broadcasted_iota(jnp.int32, (8, ROWS), 0),
        route_a, route_b, lambda v, t: v[t : t + 1, :],
    )
    S.wt[...] = hit * (match_a * share_a + match_b * share_b)
    hit_t, _, _ = chosen(
        lax.broadcasted_iota(jnp.int32, (ROWS, 8), 0), lax.broadcasted_iota(jnp.int32, (ROWS, 8), 1),
        line_a, line_b, lambda v, t: v[:, t : t + 1],
    )
    for n in range(D // 512):
        cols = slice(n * 512, n * 512 + 512)
        slotted = jnp.zeros((ROWS, 512), F32)
        for t in range(8):
            slotted = slotted + hit_t[:, t : t + 1] * moe_in[t : t + 1, cols]
        S.slots[:, cols] = slotted
    for i in range(16):
        S.out3[i] = S.slots[2 * i : 2 * i + 2, :].astype(BF16)

    column_exchange(S.out3, S.in3, "disp")
    S.in3[e] = S.out3[e]
    for d in range(1, 16):
        block = S.in3.at[mod(e + 16 - d, 16)]
        rcopy(block, block, sem_s["disp"].at[d], sem_r["disp"].at[d], (x, y, mod(e + 1, 16))).wait_recv()
    for i in range(16):
        S.slots[2 * i : 2 * i + 2, :] = S.in3[i].astype(F32)
    for h in range(2):
        S.rows[2 * own + h] = S.slots[16 * h : 16 * h + 16, :].astype(BF16)
    ag1 = RingGather(S.rows, lambda p: (b * 4 + p) * 2, 1, a, dev_a, sem_s["ag1"], sem_r["ag1"])
    ag2 = [
        RingGather(
            S.rows, lambda p, k=k: (p * 4 + k) * 2, 1, b, dev_b, sem_s["ag2"], sem_r["ag2"], 6 * i
        )
        for i, k in enumerate((a, a_left, a_right, a_opp))
    ]
    ag1.start()
    ag2[0].start()
    ag1.forward()
    ag2[0].forward()
    ag1.sides()
    ag2[1].start()
    ag2[2].start()
    ag1.opposite()
    ag2[3].start()
    for copy in local[2:5]:
        copy.wait()

    def hidden_units(bundles):
        count = len(bundles)
        tall = slice(0, count * T)
        S.acc_g[tall, :] = jnp.zeros((count * T, HU), F32)
        S.acc_u[tall, :] = jnp.zeros((count * T, HU), F32)

        @pl.loop(0, D // 1024)
        def _(n):
            cols = pl.ds(pl.multiple_of(n * 1024, 1024), 1024)
            rows = [S.rows[pl.ds(8 * p, 8), :, cols].reshape(T, 1024) for p in bundles]
            rows = rows[0] if count == 1 else jnp.concatenate(rows, axis=0)
            S.acc_g[tall, :] += dot_t(rows, S.gw[:, cols])
            S.acc_u[tall, :] += dot_t(rows, S.uw[:, cols])

        S.hidden[tall, :] = (silu(S.acc_g[tall, :]) * S.acc_u[tall, :]).astype(BF16)

    def down(bundles, chunk, target):
        tall = slice(0, len(bundles) * T)

        @pl.loop(0, WIDE // 512)
        def _(n):
            cols = pl.ds(pl.multiple_of(n * 512, 512), 512)
            wide = pl.ds(pl.multiple_of(chunk * WIDE + n * 512, 512), 512)
            result = jnp.dot(S.hidden[tall, :], S.dw[:, wide], preferred_element_type=F32)
            for k, p in enumerate(bundles):
                block = result[k * T : k * T + T].reshape(8, 16, 512)
                target[pl.ds(8 * p, 8), :, cols] = block.astype(BF16)

    parts = [getattr(S, f"y_{i}") for i in range(CHUNKS)]
    red1 = [
        RingReduce(
            parts[i], lambda p: p * 8, 4, b, dev_b, getattr(S, f"r1_{i}"), getattr(S, f"r2_{i}"),
            getattr(S, f"sm_{i}"), sem_s[f"red1_{i}"], sem_r[f"red1_{i}"],
        )
        for i in range(CHUNKS)
    ]
    red2 = [
        RingReduce(
            getattr(S, f"zin_{i}"), lambda p: p * 2, 1, a, dev_a, getattr(S, f"q1_{i}"), getattr(S, f"q2_{i}"),
            getattr(S, f"qm_{i}"), sem_s[f"red2_{i}"], sem_r[f"red2_{i}"],
        )
        for i in range(CHUNKS)
    ]
    b_right, b_left, b_opp = red1[0].right, red1[0].left, red1[0].opp

    hidden_units([b])
    ag2[1].forward()
    ag2[2].forward()
    for i in range(CHUNKS):
        down([b], i, parts[i])
    ag2[3].forward()
    for ring in ag2:
        ring.sides()
    hidden_units([b_left, b_right])
    for i in range(CHUNKS):
        down([b_left, b_right], i, parts[i])
        red1[i].start_sides()
    for ring in ag2:
        ring.opposite()
    hidden_units([b_opp])

    for i in range(CHUNKS):
        down([b_opp], i, parts[i])
        red1[i].start()

    def to_second(i):
        def store(k, value):
            getattr(S, f"zin_{i}")[k] = value

        return store

    def to_slots(i):
        def store(k, value):
            S.slots[pl.ds(pl.multiple_of(16 * k, 16), 16), i * WIDE : (i + 1) * WIDE] = value.astype(F32)

        return store

    def send_back(h):
        ret, back = getattr(S, f"ret_{h}"), getattr(S, f"back_{h}")
        half = slice(h * (D // 2), (h + 1) * (D // 2))
        for i in range(16):
            ret[i] = S.slots[2 * i : 2 * i + 2, half].astype(BF16)
        column_exchange(ret, back, f"ret_{h}")
        back[e] = ret[e]

    for i in range(CHUNKS):
        red1[i].middle()
    for i in range(CHUNKS):
        red1[i].finish(to_second(i))
        red2[i].start()
        red2[i].start_sides()
        if i >= 1:
            red2[i - 1].middle()
        if i >= 2:
            red2[i - 2].finish(to_slots(i - 2))
    send_back(0)
    red2[CHUNKS - 1].middle()
    red2[CHUNKS - 2].finish(to_slots(CHUNKS - 2))
    red2[CHUNKS - 1].finish(to_slots(CHUNKS - 1))
    send_back(1)
    for h in range(2):
        for d in range(1, 16):
            block = getattr(S, f"back_{h}").at[mod(e + 16 - d, 16)]
            rcopy(
                block, block, sem_s[f"ret_{h}"].at[d], sem_r[f"ret_{h}"].at[d], (x, y, mod(e + 1, 16))
            ).wait_recv()

    weights = S.wt[...]
    for h in range(2):
        half = slice(h * (D // 2), (h + 1) * (D // 2))
        mixed = S.hid[:, half]
        for i in range(16):
            pair_rows = getattr(S, f"back_{h}")[i].astype(F32)
            for m in range(2):
                j = 2 * i + m
                mixed = mixed + weights[:, j : j + 1] * pair_rows[m : m + 1, :]
        out_ref[:, half] = mixed.astype(BF16)

    for copy in drains:
        copy.wait_send()
    for ring in (win0, win1, mix, gat, ow1, ow2, ag1, *ag2, *red1, *red2):
        ring.drain()
    for d in range(1, 16):

        @pl.when(s + d < 16)
        def _():
            sum_copy(d).wait_send()
            state_copy(d).wait_send()


def local_step(
    tokens, norm_gain, in_weight, conv_weight, conv_bias, proj_weight, step_weight, step_bias, decay_log,
    skip_gain, out_weight, moe_gain, router_weight, routes, gate_weight, up_weight, down_weight,
):
    operands = (
        tokens, norm_gain[None], in_weight, conv_weight, conv_bias[None],
        jnp.transpose(proj_weight), step_weight, step_bias[None], jnp.transpose(decay_log), skip_gain[None],
        out_weight.reshape(2, C // 2, FD), moe_gain[None], jnp.transpose(router_weight), jnp.transpose(routes),
        jnp.transpose(gate_weight[0]), jnp.transpose(up_weight[0]), down_weight[0],
    )
    spaces = {"v": pltpu.VMEM, "a": pl.ANY}
    return pl.pallas_call(
        kernel,
        out_shape=jax.ShapeDtypeStruct((8, D), BF16),
        in_specs=[pl.BlockSpec(memory_space=spaces[kind]) for _, kind in INPUTS],
        out_specs=pl.BlockSpec(memory_space=pltpu.VMEM),
        scratch_shapes=[pltpu.VMEM(shape, dtype) for shape, dtype in SCRATCH.values()]
        + [pltpu.SemaphoreType.DMA((count,)) for count in SEMS.values()] * 2,
        compiler_params=pltpu.CompilerParams(
            collective_id=0, has_side_effects=True, vmem_limit_bytes=60 * 1024 * 1024
        ),
    )(*operands)


def solution(mesh):
    split = Mesh(mesh.devices.reshape(4, 4, mesh.shape["expert"]), ("seq_0", "seq_1", "expert"))
    in_specs = (
        P(SEQ, None),
        P(),
        P(SEQ, None, "expert"),
        P(None, "expert"),
        P("expert"),
        P("expert", None),
        P(None, "expert"),
        P("expert"),
        P("expert", None),
        P("expert"),
        P("expert", SEQ),
        P(),
        P(),
        P(SEQ_EXPERT, None),
        P("expert", None, SEQ),
        P("expert", None, SEQ),
        P("expert", SEQ, None),
    )
    out_specs = P(SEQ_EXPERT, None)
    return jax.shard_map(local_step, mesh=split, in_specs=in_specs, out_specs=out_specs, check_vma=False)
```

```python
import types

import jax
import jax.numpy as jnp
from jax import lax
from jax.experimental import pallas as pl
from jax.experimental.pallas import tpu as pltpu
from jax.sharding import Mesh
from jax.sharding import PartitionSpec as P

SEQ = ("seq_0", "seq_1")
SEQ_EXPERT = ("seq_0", "seq_1", "expert")
EPSILON = 1e-06
F32 = jnp.float32
BF16 = jnp.bfloat16

D = 4096
T = 128
C = 512
FD = 256
N = 16
RANK = 256
HU = 448
ROWS = 32


def mod(v, n):
    return lax.rem(v, n)


def rcopy(src, dst, send, recv, device):
    return pltpu.make_async_remote_copy(
        src_ref=src,
        dst_ref=dst,
        send_sem=send,
        recv_sem=recv,
        device_id=device,
        device_id_type=pl.DeviceIdType.MESH,
    )


def dot_t(left, right):
    return lax.dot_general(left, right, (((1,), (1,)), ((), ())), preferred_element_type=F32)


def silu(v):
    return v / (1.0 + jnp.exp(-v))


class RingGather:
    def __init__(self, buf, base, half, pos, dev, send, recv, offset=0):
        self.buf, self.base, self.half, self.dev = buf, base, half, dev
        self.send, self.recv, self.offset = send, recv, offset
        self.pos, self.right, self.left, self.opp = pos, mod(pos + 1, 4), mod(pos + 3, 4), mod(pos + 2, 4)
        self.started = []

    def part(self, pos, h):
        return self.buf.at[pl.ds(self.base(pos) + h * self.half, self.half)]

    def go(self, pos, h, to, k):
        block = self.part(pos, h)
        k = k + self.offset
        copy = rcopy(block, block, self.send.at[k], self.recv.at[k], self.dev(to))
        copy.start()
        self.started.append(copy)

    def arrived(self, pos, h, k):
        block = self.part(pos, h)
        k = k + self.offset
        rcopy(block, block, self.send.at[k], self.recv.at[k], self.dev(self.right)).wait_recv()

    def start(self):
        self.go(self.pos, 0, self.right, 0)
        self.go(self.pos, 1, self.left, 3)
        self.go(self.pos, 1, self.right, 1)
        self.go(self.pos, 0, self.left, 2)

    def forward(self):
        self.arrived(self.left, 0, 0)
        self.go(self.left, 0, self.right, 4)
        self.arrived(self.right, 1, 3)
        self.go(self.right, 1, self.left, 5)

    def sides(self):
        self.arrived(self.left, 1, 1)
        self.arrived(self.right, 0, 2)

    def opposite(self):
        self.arrived(self.opp, 0, 4)
        self.arrived(self.opp, 1, 5)

    def drain(self):
        for copy in self.started:
            copy.wait_send()


class RingReduce:
    def __init__(self, part, base, half, pos, dev, first, second, summed, send, recv):
        self.buf, self.base, self.half, self.dev = part, base, half, dev
        self.first, self.second, self.summed = first, second, summed
        self.send, self.recv = send, recv
        self.pos, self.right, self.left, self.opp = pos, mod(pos + 1, 4), mod(pos + 3, 4), mod(pos + 2, 4)
        self.started = []

    def part(self, pos, h):
        return self.buf.at[pl.ds(self.base(pos) + h * self.half, self.half)]

    def go(self, src, dst, to, k):
        copy = rcopy(src, dst, self.send.at[k], self.recv.at[k], self.dev(to))
        copy.start()
        self.started.append(copy)

    def arrived(self, dst, k):
        rcopy(dst, dst, self.send.at[k], self.recv.at[k], self.dev(self.right)).wait_recv()

    def start(self):
        self.go(self.part(self.opp, 0), self.first.at[0], self.right, 0)
        self.go(self.part(self.opp, 1), self.first.at[1], self.left, 1)

    def start_sides(self):
        h = self.half
        self.go(self.part(self.right, 1), self.second.at[0, pl.ds(h, h)], self.right, 2)
        self.go(self.part(self.left, 0), self.second.at[1, pl.ds(0, h)], self.left, 3)

    def middle(self):
        h = self.half
        for side, (owner, which) in enumerate(((self.right, 0), (self.left, 1))):
            self.arrived(self.first.at[side], side)
            at = self.base(owner) + which * h

            @pl.loop(0, h)
            def _(i):
                total = self.buf[at + i].astype(F32) + self.first[side, i].astype(F32)
                self.summed[side, i] = total.astype(BF16)

            self.go(self.summed.at[side], self.second.at[side, pl.ds(which * h, h)], owner, 4 + side)

    def finish(self, store):
        h = self.half
        self.arrived(self.second.at[0, pl.ds(h, h)], 2)
        self.arrived(self.second.at[1, pl.ds(0, h)], 3)
        self.arrived(self.second.at[0, pl.ds(0, h)], 4)
        self.arrived(self.second.at[1, pl.ds(h, h)], 5)
        at = self.base(self.pos)

        @pl.loop(0, 2 * h)
        def _(i):
            total = self.buf[at + i].astype(F32) + self.second[0, i].astype(F32)
            store(i, (total + self.second[1, i].astype(F32)).astype(BF16))

    def drain(self):
        for copy in self.started:
            copy.wait_send()


INPUTS = (
    ("tokens", "v"), ("norm_gain", "v"), ("in_weight", "a"), ("conv_weight", "v"), ("conv_bias", "v"),
    ("proj_weight", "v"), ("step_weight", "v"), ("step_bias", "v"), ("decay_log", "v"), ("skip_gain", "v"),
    ("out_weight", "a"), ("moe_gain", "v"), ("router_weight", "v"), ("routes", "v"),
    ("gate_weight", "a"), ("up_weight", "a"), ("down_weight", "a"),
)

CHUNKS = 4
WIDE = D // CHUNKS

SCRATCH = {
    "normed": ((16, T, FD), BF16),
    "tok_g": ((16, T, FD), BF16),
    "wraw": ((FD, 2, C), BF16),
    "wg": ((16, FD // 2, C), BF16),
    "part_0": ((8, T // 2, C), BF16),
    "part_1": ((8, T // 2, C), BF16),
    "m1_0": ((2, 1, T // 2, C), BF16),
    "m2_0": ((2, 2, T // 2, C), BF16),
    "ms_0": ((2, 1, T // 2, C), BF16),
    "m1_1": ((2, 1, T // 2, C), BF16),
    "m2_1": ((2, 2, T // 2, C), BF16),
    "ms_1": ((2, 1, T // 2, C), BF16),
    "padf": ((T + 16, C), F32),
    "gate": ((T, C), F32),
    "hsrc": ((16, C), BF16),
    "hdst": ((16, C), BF16),
    "act": ((T, C), BF16),
    "feat": ((16, 8, 384), BF16),
    "frecv": ((16, 8, 384), BF16),
    "fsum": ((8, 384), BF16),
    "fall": ((16, 8, 384), BF16),
    "step": ((T, C), F32),
    "drive": ((T, C), F32),
    "maps_t": ((ROWS, T), F32),
    "y": ((T, C), F32),
    "stx": ((N, C), BF16),
    "stall": ((16, N, C), BF16),
    "sumx": ((8, C), F32),
    "sumall": ((16, 8, C), F32),
    "passed": ((16, N, C), F32),
    "gated": ((T, C), BF16),
    "ow": ((32, C // 2, FD), BF16),
    **{
        f"{name}_{h}": (shape, BF16)
        for h in range(2)
        for name, shape in {
            "outp": (16, 8, D // 2), "pair": (8, 8, D // 2), "zs": (8, 8, D // 2), "zrecv": (8, 8, D // 2),
            "zs4": (2, 8, D // 4), "z4r": (2, 8, D // 4),
        }.items()
    },
    "hid": ((8, D), F32),
    "wt": ((8, ROWS), F32),
    "slots": ((ROWS, D), F32),
    **{
        f"{name}_{h}": ((*shape, D // 2), BF16)
        for h in range(2)
        for name, shape in {"out": (16, 2), "in": (16, 2), "rows": (32, 16)}.items()
    },
    "gw": ((HU, D), BF16),
    "uw": ((HU, D), BF16),
    "dw": ((HU, D), BF16),
    "acc_g": ((2 * T, HU), F32),
    "acc_u": ((2 * T, HU), F32),
    "hidden": ((2 * T, HU), BF16),
    **{
        f"{name}_{chunk}": ((*shape, 16, WIDE), BF16)
        for chunk in range(CHUNKS)
        for name, shape in {
            "y": (32,), "r1": (2, 4), "r2": (2, 8), "sm": (2, 4), "zin": (8,), "q1": (2, 1), "q2": (2, 2), "qm": (2, 1),
        }.items()
    },
    "ret_0": ((16, 2, D // 2), BF16),
    "ret_1": ((16, 2, D // 2), BF16),
    "back_0": ((16, 2, D // 2), BF16),
    "back_1": ((16, 2, D // 2), BF16),
}

SEMS = {
    "local": 6,
    "tok": 6, "win0": 6, "win1": 6, "mix": 6, "gat": 6, "halo": 1, "f1": 16, "f2": 16, "st": 16, "sum": 16, "ow1": 6, "ow2": 6,
    "pair_0": 1, "pair_1": 1, "z_0": 8, "z_1": 8, "z4_0": 2, "z4_1": 2, "disp_0": 16, "disp_1": 16, "ag1_0": 6, "ag1_1": 6, "ag2_0": 24, "ag2_1": 24,
    **{f"{name}_{chunk}": 6 for name in ("red1", "red2") for chunk in range(CHUNKS)},
    "ret_0": 16, "ret_1": 16,
}

FAR_16 = (8, 7, 9, 6, 10, 5, 11, 4, 12, 3, 13, 2, 14, 1, 15)


def kernel(*refs):
    count = len(INPUTS)
    I = types.SimpleNamespace(**{name: r for (name, _), r in zip(INPUTS, refs[:count])})
    out_ref = refs[count]
    rest = refs[count + 1 :]
    S = types.SimpleNamespace(**dict(zip(SCRATCH, rest[: len(SCRATCH)])))
    rest = rest[len(SCRATCH) :]
    sem_s = dict(zip(SEMS, rest[: len(SEMS)]))
    sem_r = dict(zip(SEMS, rest[len(SEMS) :]))

    x, y, e = lax.axis_index("seq_0"), lax.axis_index("seq_1"), lax.axis_index("expert")
    c, z = mod(e, 2), e // 2
    s = 4 * x + y
    a = c * x + (1 - c) * y
    b = (1 - c) * x + c * y

    def dev_a(k):
        return (x + c * (k - x), y + (1 - c) * (k - y), e)

    def dev_b(k):
        return (x + (1 - c) * (k - x), y + c * (k - y), e)

    def dev_s(k):
        return (k // 4, mod(k, 4), e)

    drains = []

    def column_exchange(src, dst, name):
        send, recv = sem_s[name], sem_r[name]

        def piece(d):
            to = mod(e + d, 16)
            finish_later(rcopy(src.at[to], dst.at[e], send.at[d], recv.at[d], (x, y, to)))

        for d in FAR_16:
            piece(d)

    def finish_later(copy):
        copy.start()
        drains.append(copy)

    barrier = pltpu.get_barrier_semaphore()
    for d in range(1, 16):
        pl.semaphore_signal(barrier, inc=1, device_id=(x, y, mod(e + d, 16)), device_id_type=pl.DeviceIdType.MESH)
        pl.semaphore_signal(barrier, inc=1, device_id=dev_s(mod(s + d, 16)), device_id_type=pl.DeviceIdType.MESH)

    own = b * 4 + a
    local = [
        pltpu.make_async_copy(I.in_weight, S.wraw, sem_s["local"].at[0]),
        pltpu.make_async_copy(I.out_weight, S.ow.at[pl.ds(2 * own, 2)], sem_s["local"].at[1]),
        pltpu.make_async_copy(I.gate_weight, S.gw, sem_s["local"].at[2]),
        pltpu.make_async_copy(I.up_weight, S.uw, sem_s["local"].at[3]),
        pltpu.make_async_copy(I.down_weight, S.dw, sem_s["local"].at[4]),
    ]
    for copy in (local[0], local[1]):
        copy.start()

    gain = I.norm_gain[...]

    @pl.loop(0, T // 16)
    def _(i):
        rows = pl.ds(pl.multiple_of(i * 16, 16), 16)
        v = I.tokens[rows, :].astype(F32)
        inverse = lax.rsqrt(jnp.mean(v * v, axis=-1, keepdims=True) + EPSILON)
        normed = (v * inverse * gain).astype(BF16)
        for j in range(16):
            k = (1 - c) * (j % 4) + c * (j // 4)
            q = (1 - c) * (j // 4) + c * (j % 4)
            S.normed[4 * k + q, rows, :] = normed[:, j * FD : (j + 1) * FD]

    local[0].wait()
    for p in range(2):
        for h in range(2):
            S.wg[8 * p + 2 * b + h] = S.wraw[128 * h : 128 * h + 128, p, :]
    pl.semaphore_wait(barrier, 30)
    win0 = RingGather(S.wg, lambda p: 2 * p, 1, b, dev_b, sem_s["win0"], sem_r["win0"])
    win1 = RingGather(S.wg, lambda p: 8 + 2 * p, 1, b, dev_b, sem_s["win1"], sem_r["win1"])
    win0.start()

    a_right, a_left, a_opp = mod(a + 1, 4), mod(a + 3, 4), mod(a + 2, 4)

    def tok_copy(src, dst, k, to):
        return rcopy(src, dst, sem_s["tok"].at[k], sem_r["tok"].at[k], dev_a(to))

    finish_later(tok_copy(S.normed.at[pl.ds(4 * a_opp, 4)], S.tok_g.at[pl.ds(4 * a, 4)], 4, a_opp))
    finish_later(tok_copy(S.normed.at[pl.ds(4 * a_right, 4)], S.tok_g.at[pl.ds(4 * a, 4)], 2, a_right))
    finish_later(tok_copy(S.normed.at[pl.ds(4 * a_left, 4)], S.tok_g.at[pl.ds(4 * a, 4)], 3, a_left))
    win0.forward()
    win0.sides()
    win0.opposite()
    for block, k in (
        (S.tok_g.at[pl.ds(4 * a_left, 4)], 2), (S.tok_g.at[pl.ds(4 * a_right, 4)], 3),
        (S.tok_g.at[pl.ds(4 * a_opp, 4)], 4),
    ):
        tok_copy(block, block, k, a_right).wait_recv()

    win1.start()
    local[1].wait()
    ow1 = RingGather(S.ow, lambda p: (b * 4 + p) * 2, 1, a, dev_a, sem_s["ow1"], sem_r["ow1"])
    ow1.start()

    def project(branch, part, k, source):
        @pl.loop(0, C // 256)
        def _(n):
            cols = pl.ds(pl.multiple_of(n * 256, 256), 256)
            total = jnp.zeros((T, 256), F32)
            for q in range(4):
                at = 8 * branch + 2 * q
                weight = S.wg[at : at + 2, :, cols].reshape(FD, 256)
                total = total + jnp.dot(source[4 * k + q], weight, preferred_element_type=F32)
            part[pl.ds(2 * k, 2), :, cols] = total.reshape(2, T // 2, 256).astype(BF16)

    def project_all(branch, part, ring):
        project(branch, part, a_opp, S.tok_g)
        ring.start()
        project(branch, part, a_right, S.tok_g)
        project(branch, part, a_left, S.tok_g)
        ring.start_sides()
        project(branch, part, a, S.normed)

    mix = RingReduce(
        S.part_0, lambda p: 2 * p, 1, a, dev_a, S.m1_0, S.m2_0, S.ms_0, sem_s["mix"], sem_r["mix"]
    )
    gat = RingReduce(
        S.part_1, lambda p: 2 * p, 1, a, dev_a, S.m1_1, S.m2_1, S.ms_1, sem_s["gat"], sem_r["gat"]
    )
    project_all(0, S.part_0, mix)
    mix.middle()
    win1.forward()
    ow1.forward()

    def to_mixer(i, value):
        S.padf[pl.ds(pl.multiple_of(16 + i * (T // 2), 16), T // 2), :] = value.astype(F32)

    mix.finish(to_mixer)

    S.hsrc[...] = S.padf[T : T + 16, :].astype(BF16)
    finish_later(
        rcopy(S.hsrc, S.hdst, sem_s["halo"].at[0], sem_r["halo"].at[0], dev_s(mod(s + 1, 16)))
    )

    def convolve(i):
        window = S.padf[pl.ds(pl.multiple_of(i * 16, 16), 32), :]
        total = I.conv_bias[...] + jnp.zeros((16, C), F32)
        for tap in range(4):
            total = total + I.conv_weight[tap : tap + 1, :] * window[13 + tap : 29 + tap, :]
        S.act[pl.ds(pl.multiple_of(i * 16, 16), 16), :] = silu(total).astype(BF16)

    pl.loop(1, T // 16)(convolve)
    rcopy(S.hdst, S.hdst, sem_s["halo"].at[0], sem_r["halo"].at[0], dev_s(mod(s + 1, 16))).wait_recv()
    first = jnp.zeros((16, C), jnp.int32) + s
    S.padf[0:16, :] = jnp.where(first > 0, S.hdst[...].astype(F32), 0.0)
    convolve(0)

    def in_three(v):
        high = v.astype(BF16)
        rest = v - high.astype(F32)
        middle = rest.astype(BF16)
        return high, middle, (rest - middle.astype(F32)).astype(BF16)

    full = dot_t(S.act[...], I.proj_weight[...])
    S.feat[:, :, RANK:] = jnp.zeros((16, 8, 128), BF16)
    S.feat[:, :, :RANK] = full[:, :RANK].reshape(16, 8, RANK).astype(BF16)
    for k, term in enumerate(in_three(full[:, RANK:].reshape(16, 8, 2 * N))):
        S.feat[:, :, RANK + 32 * k : RANK + 32 * k + 32] = term
    for d in FAR_16:
        to = mod(e + d, 16)
        finish_later(rcopy(S.feat.at[to], S.frecv.at[e], sem_s["f1"].at[d], sem_r["f1"].at[d], (x, y, to)))
    ow1.sides()
    ow1.opposite()
    ow2 = RingGather(S.ow, lambda p: p * 8, 4, b, dev_b, sem_s["ow2"], sem_r["ow2"])
    ow2.start()
    win1.sides()
    win1.opposite()
    project_all(1, S.part_1, gat)
    S.frecv[e] = S.feat[e]
    for d in range(1, 16):
        block = S.frecv.at[mod(e + 16 - d, 16)]
        rcopy(block, block, sem_s["f1"].at[d], sem_r["f1"].at[d], (x, y, mod(e + 1, 16))).wait_recv()
    total = S.frecv[0].astype(F32)
    for d in range(1, 16):
        total = total + S.frecv[d].astype(F32)
    maps = total[:, RANK : RANK + 32] + total[:, RANK + 32 : RANK + 64] + total[:, RANK + 64 : RANK + 96]
    S.fsum[:, :RANK] = total[:, :RANK].astype(BF16)
    S.fsum[:, RANK:] = jnp.zeros((8, 128), BF16)
    for k, term in enumerate(in_three(maps)):
        S.fsum[:, RANK + 32 * k : RANK + 32 * k + 32] = term
    for d in FAR_16:
        to = mod(e + d, 16)
        finish_later(rcopy(S.fsum, S.fall.at[e], sem_s["f2"].at[d], sem_r["f2"].at[d], (x, y, to)))
    S.fall[e] = S.fsum[...]
    gat.middle()

    def to_gate(i, value):
        S.gate[pl.ds(pl.multiple_of(i * (T // 2), 16), T // 2), :] = value.astype(F32)

    gat.finish(to_gate)
    for d in range(1, 16):
        block = S.fall.at[mod(e + 16 - d, 16)]
        rcopy(block, block, sem_s["f2"].at[d], sem_r["f2"].at[d], (x, y, mod(e + 1, 16))).wait_recv()
    low = S.fall[:, :, :RANK].astype(F32).reshape(T, RANK).astype(BF16)
    upright_maps = jnp.transpose(S.fall[:, :, RANK:].astype(F32).reshape(T, 128))
    S.maps_t[...] = upright_maps[0:32, :] + upright_maps[32:64, :] + upright_maps[64:96, :]
    raw = jnp.dot(low, I.step_weight[...], preferred_element_type=F32) + I.step_bias[...]
    S.step[...] = jnp.maximum(raw, 0.0) + jnp.log1p(jnp.exp(-jnp.abs(raw)))
    S.drive[...] = S.step[...] * S.act[...].astype(F32)

    rate = -jnp.exp(I.decay_log[...])

    def scan(start, emit):
        def block(i, state):
            rows = pl.ds(pl.multiple_of(i * 8, 8), 8)
            steps, drives = S.step[rows, :], S.drive[rows, :]
            maps = pltpu.roll(S.maps_t[...], mod(T - 8 * i, T), 1)
            lines = []
            for t in range(8):
                state = jnp.exp(steps[t : t + 1, :] * rate) * state + drives[t : t + 1, :] * maps[:N, t : t + 1]
                if emit:
                    lines.append(jnp.sum(state * maps[N:, t : t + 1], axis=0, keepdims=True))
            if emit:
                S.y[rows, :] = jnp.concatenate(lines, axis=0)
            return state

        return lax.fori_loop(0, T // 8, block, start)

    def sum_copy(d):
        to = dev_s(mod(s + d, 16))
        return rcopy(S.sumx, S.sumall.at[s], sem_s["sum"].at[d], sem_r["sum"].at[d], to)

    def state_copy(d):
        to = dev_s(mod(s + d, 16))
        return rcopy(S.stx, S.stall.at[s], sem_s["st"].at[d], sem_r["st"].at[d], to)

    def to_later(copy_of):
        for d in range(15, 0, -1):

            @pl.when(s + d < 16)
            def _():
                copy_of(d).start()

    for copy in local[2:5]:
        copy.start()
    S.sumx[...] = jnp.broadcast_to(jnp.sum(S.step[...], axis=0, keepdims=True), (8, C))
    to_later(sum_copy)
    zero_state = jnp.zeros((N, C), F32)
    S.stx[...] = scan(zero_state, False).astype(BF16)
    to_later(state_copy)

    ow2.forward()
    for d in range(1, 16):

        @pl.when(s - d >= 0)
        def _():
            block = S.sumall.at[mod(s + 16 - d, 16)]
            rcopy(block, block, sem_s["sum"].at[d], sem_r["sum"].at[d], dev_s(mod(s + d, 16))).wait_recv()

    def passed(i, steps):
        k = s - 1 - i
        S.passed[k] = jnp.exp(rate * steps)
        return steps + S.sumall[k, 0:1, :]

    lax.fori_loop(0, s, passed, jnp.zeros((1, C), F32))
    for d in range(1, 16):

        @pl.when(s - d >= 0)
        def _():
            block = S.stall.at[mod(s + 16 - d, 16)]
            rcopy(block, block, sem_s["st"].at[d], sem_r["st"].at[d], dev_s(mod(s + d, 16))).wait_recv()

    def compose(k, state):
        return state + S.passed[k] * S.stall[k].astype(F32)

    scan(lax.fori_loop(0, s, compose, zero_state), True)

    @pl.loop(0, T // 16)
    def _(i):
        rows = pl.ds(pl.multiple_of(i * 16, 16), 16)
        scanned = S.y[rows, :] + I.skip_gain[...] * S.act[rows, :].astype(F32)
        S.gated[rows, :] = (scanned * silu(S.gate[rows, :])).astype(BF16)

    ow2.sides()
    ow2.opposite()

    other = e + 1 - 2 * c

    class Half:
        def __init__(self, h):
            self.h = h
            for name in ("outp", "pair", "zs", "zrecv", "zs4", "z4r"):
                setattr(self, name, getattr(S, f"{name}_{h}"))

        def sems(self, name, k):
            return sem_s[f"{name}_{self.h}"].at[k], sem_r[f"{name}_{self.h}"].at[k]

        def multiply(self):
            @pl.loop(0, 8)
            def _(n):
                column = 8 * self.h + n
                at = (1 - c) * column + c * (4 * mod(column, 4) + column // 4)
                weight = S.ow[pl.ds(2 * at, 2)].reshape(C, FD)
                total = jnp.dot(S.gated[...], weight, preferred_element_type=F32).reshape(8, 2, 8, FD)
                cols = pl.ds(pl.multiple_of(n * FD, FD), FD)
                self.outp[0:8, :, cols] = total[:, 0].astype(BF16)
                self.outp[8:16, :, cols] = total[:, 1].astype(BF16)

            self.pair_copy = rcopy(
                self.outp.at[pl.ds(8 * (1 - c), 8)], self.pair, *self.sems("pair", 0), (x, y, other)
            )
            finish_later(self.pair_copy)

        def chip_sum(self, zz):
            return self.outp[8 * c + zz].astype(F32) + self.pair[zz].astype(F32)

        def z_copy(self, d):
            zz = mod(z + d, 8)
            finish_later(rcopy(self.zs.at[zz], self.zrecv.at[z], *self.sems("z", d), (x, y, 2 * zz + c)))

        def start(self):
            self.pair_copy.wait_recv()
            across = self.chip_sum(mod(z + 4, 8)).astype(BF16)
            for k, step in ((0, 2), (1, 14)):
                self.zs4[k] = across[:, k * (D // 4) : (k + 1) * (D // 4)]
                finish_later(
                    rcopy(self.zs4.at[k], self.z4r.at[k], *self.sems("z4", k), (x, y, mod(e + step, 16)))
                )
            for d in (2, 6, 1, 7):
                zz = mod(z + d, 8)
                self.zs[zz] = self.chip_sum(zz).astype(BF16)
                self.z_copy(d)

        def join(self):
            for h, d in ((0, 3), (1, 5)):
                zz = mod(z + d, 8)
                plain = self.chip_sum(zz)
                rcopy(self.z4r.at[h], self.z4r.at[h], *self.sems("z4", h), (x, y, other)).wait_recv()
                arrived = self.z4r[h].astype(F32)
                for k in range(2):
                    part = slice(k * (D // 4), (k + 1) * (D // 4))
                    value = plain[:, part] + arrived if k == h else plain[:, part]
                    self.zs[zz, :, part] = value.astype(BF16)
                self.z_copy(d)

        def finish(self):
            total = self.chip_sum(z)
            for d in (1, 2, 3, 5, 6, 7):
                block = self.zrecv.at[mod(z + 8 - d, 8)]
                rcopy(block, block, *self.sems("z", d), (x, y, other)).wait_recv()
            for d in (1, 2, 3, 5, 6, 7):
                total = total + self.zrecv[mod(z + d, 8)].astype(F32)
            return total

    halves = [Half(h) for h in range(2)]
    for half in halves:
        half.multiply()
    for half in halves:
        half.start()
    for half in halves:
        half.join()
    total = jnp.concatenate([half.finish() for half in halves], axis=1)

    both = I.tokens[pl.ds(pl.multiple_of(16 * z, 16), 16), :].astype(F32)
    core = jnp.zeros((8, D), jnp.int32) + c
    mine = jnp.where(core == 0, both[:8, :], both[8:, :])
    hid = (mine + total).astype(BF16).astype(F32)
    S.hid[...] = hid
    inverse = lax.rsqrt(jnp.mean(hid * hid, axis=-1, keepdims=True) + EPSILON)
    moe_in = (hid * inverse * I.moe_gain[...]).astype(BF16).astype(F32)
    twice = jnp.concatenate([moe_in, moe_in], axis=0).astype(BF16)
    logits = dot_t(twice, I.router_weight[...])[:8, :]

    ids = lax.broadcasted_iota(jnp.int32, (8, 16), 1)
    line_a, line_b = I.routes[0:1, :], I.routes[1:2, :]
    diagonal = lax.broadcasted_iota(jnp.int32, (8, 8), 0) == lax.broadcasted_iota(jnp.int32, (8, 8), 1)

    def upright(line):
        lines = jnp.where(diagonal, line.astype(F32), 0.0)
        return jnp.sum(lines, axis=1, keepdims=True).astype(jnp.int32)

    route_a, route_b = upright(line_a), upright(line_b)
    picked_a = jnp.sum(jnp.where(route_a == ids, logits, 0.0), axis=1, keepdims=True)
    picked_b = jnp.sum(jnp.where(route_b == ids, logits, 0.0), axis=1, keepdims=True)
    share_a = 1.0 / (1.0 + jnp.exp(picked_b - picked_a))
    share_b = 1.0 - share_a

    def chosen(slot, token, ra, rb, row_of):
        expert, slot_no = slot // 2, mod(slot, 2)
        match_a = jnp.where(ra == expert, 1.0, 0.0)
        match_b = jnp.where(rb == expert, 1.0, 0.0)
        named = match_a + match_b
        before = jnp.zeros_like(named)
        for t in range(7):
            before = before + jnp.where(token > t, row_of(named, t), 0.0)
        hit = jnp.where(before == slot_no.astype(F32), named, 0.0)
        return hit, match_a, match_b

    hit, match_a, match_b = chosen(
        lax.broadcasted_iota(jnp.int32, (8, ROWS), 1), lax.broadcasted_iota(jnp.int32, (8, ROWS), 0),
        route_a, route_b, lambda v, t: v[t : t + 1, :],
    )
    S.wt[...] = hit * (match_a * share_a + match_b * share_b)
    hit_t, _, _ = chosen(
        lax.broadcasted_iota(jnp.int32, (ROWS, 8), 0), lax.broadcasted_iota(jnp.int32, (ROWS, 8), 1),
        line_a, line_b, lambda v, t: v[:, t : t + 1],
    )
    for n in range(D // 512):
        cols = slice(n * 512, n * 512 + 512)
        slotted = jnp.zeros((ROWS, 512), F32)
        for t in range(8):
            slotted = slotted + hit_t[:, t : t + 1] * moe_in[t : t + 1, cols]
        S.slots[:, cols] = slotted

    column_halves = [slice(h * (D // 2), (h + 1) * (D // 2)) for h in range(2)]
    slots_out, slots_in, rows_of = (S.out_0, S.out_1), (S.in_0, S.in_1), (S.rows_0, S.rows_1)
    for h in range(2):
        for i in range(16):
            slots_out[h][i] = S.slots[2 * i : 2 * i + 2, column_halves[h]].astype(BF16)
        column_exchange(slots_out[h], slots_in[h], f"disp_{h}")
        slots_in[h][e] = slots_out[h][e]
    ag1, ag2 = [], []
    for h in range(2):
        ag1.append(
            RingGather(
                rows_of[h], lambda p: (b * 4 + p) * 2, 1, a, dev_a, sem_s[f"ag1_{h}"], sem_r[f"ag1_{h}"]
            )
        )
        ag2.append(
            [
                RingGather(
                    rows_of[h], lambda p, k=k: (p * 4 + k) * 2, 1, b, dev_b,
                    sem_s[f"ag2_{h}"], sem_r[f"ag2_{h}"], 6 * i,
                )
                for i, k in enumerate((a, a_left, a_right, a_opp))
            ]
        )
    for h in range(2):
        for d in range(1, 16):
            block = slots_in[h].at[mod(e + 16 - d, 16)]
            rcopy(
                block, block, sem_s[f"disp_{h}"].at[d], sem_r[f"disp_{h}"].at[d], (x, y, mod(e + 1, 16))
            ).wait_recv()
        for i in range(16):
            S.slots[2 * i : 2 * i + 2, column_halves[h]] = slots_in[h][i].astype(F32)
        for k in range(2):
            rows_of[h][2 * own + k] = S.slots[16 * k : 16 * k + 16, column_halves[h]].astype(BF16)
        ag1[h].start()
        ag2[h][0].start()
    for h in range(2):
        ag1[h].forward()
        ag2[h][0].forward()
    for h in range(2):
        ag1[h].sides()
        ag2[h][1].start()
        ag2[h][2].start()
    for h in range(2):
        ag1[h].opposite()
        ag2[h][3].start()
    for copy in local[2:5]:
        copy.wait()

    def hidden_units(bundles):
        count = len(bundles)
        tall = slice(0, count * T)
        S.acc_g[tall, :] = jnp.zeros((count * T, HU), F32)
        S.acc_u[tall, :] = jnp.zeros((count * T, HU), F32)

        for h in range(2):

            @pl.loop(0, D // 2048)
            def _(n):
                cols = pl.ds(pl.multiple_of(n * 1024, 1024), 1024)
                wide = pl.ds(pl.multiple_of(h * (D // 2) + n * 1024, 1024), 1024)
                rows = [rows_of[h][pl.ds(8 * p, 8), :, cols].reshape(T, 1024) for p in bundles]
                rows = rows[0] if count == 1 else jnp.concatenate(rows, axis=0)
                S.acc_g[tall, :] += dot_t(rows, S.gw[:, wide])
                S.acc_u[tall, :] += dot_t(rows, S.uw[:, wide])

        S.hidden[tall, :] = (silu(S.acc_g[tall, :]) * S.acc_u[tall, :]).astype(BF16)

    def down(bundles, chunk, target):
        tall = slice(0, len(bundles) * T)

        @pl.loop(0, WIDE // 512)
        def _(n):
            cols = pl.ds(pl.multiple_of(n * 512, 512), 512)
            wide = pl.ds(pl.multiple_of(chunk * WIDE + n * 512, 512), 512)
            result = jnp.dot(S.hidden[tall, :], S.dw[:, wide], preferred_element_type=F32)
            for k, p in enumerate(bundles):
                block = result[k * T : k * T + T].reshape(8, 16, 512)
                target[pl.ds(8 * p, 8), :, cols] = block.astype(BF16)

    parts = [getattr(S, f"y_{i}") for i in range(CHUNKS)]
    red1 = [
        RingReduce(
            parts[i], lambda p: p * 8, 4, b, dev_b, getattr(S, f"r1_{i}"), getattr(S, f"r2_{i}"),
            getattr(S, f"sm_{i}"), sem_s[f"red1_{i}"], sem_r[f"red1_{i}"],
        )
        for i in range(CHUNKS)
    ]
    red2 = [
        RingReduce(
            getattr(S, f"zin_{i}"), lambda p: p * 2, 1, a, dev_a, getattr(S, f"q1_{i}"), getattr(S, f"q2_{i}"),
            getattr(S, f"qm_{i}"), sem_s[f"red2_{i}"], sem_r[f"red2_{i}"],
        )
        for i in range(CHUNKS)
    ]
    b_right, b_left, b_opp = red1[0].right, red1[0].left, red1[0].opp

    hidden_units([b])
    for h in range(2):
        ag2[h][1].forward()
        ag2[h][2].forward()
    for i in range(CHUNKS):
        down([b], i, parts[i])
    for h in range(2):
        ag2[h][3].forward()
    for ring in ag2[0] + ag2[1]:
        ring.sides()
    hidden_units([b_left, b_right])
    for i in range(CHUNKS):
        down([b_left, b_right], i, parts[i])
        red1[i].start_sides()
    for ring in ag2[0] + ag2[1]:
        ring.opposite()
    hidden_units([b_opp])

    for i in range(CHUNKS):
        down([b_opp], i, parts[i])
        red1[i].start()

    def to_second(i):
        def store(k, value):
            getattr(S, f"zin_{i}")[k] = value

        return store

    def to_slots(i):
        def store(k, value):
            S.slots[pl.ds(pl.multiple_of(16 * k, 16), 16), i * WIDE : (i + 1) * WIDE] = value.astype(F32)

        return store

    def send_back(h):
        ret, back = getattr(S, f"ret_{h}"), getattr(S, f"back_{h}")
        half = slice(h * (D // 2), (h + 1) * (D // 2))
        for i in range(16):
            ret[i] = S.slots[2 * i : 2 * i + 2, half].astype(BF16)
        column_exchange(ret, back, f"ret_{h}")
        back[e] = ret[e]

    for i in range(CHUNKS):
        red1[i].middle()
    for i in range(CHUNKS):
        red1[i].finish(to_second(i))
        red2[i].start()
        red2[i].start_sides()
        if i >= 1:
            red2[i - 1].middle()
        if i >= 2:
            red2[i - 2].finish(to_slots(i - 2))
    send_back(0)
    red2[CHUNKS - 1].middle()
    red2[CHUNKS - 2].finish(to_slots(CHUNKS - 2))
    red2[CHUNKS - 1].finish(to_slots(CHUNKS - 1))
    send_back(1)
    for h in range(2):
        for d in range(1, 16):
            block = getattr(S, f"back_{h}").at[mod(e + 16 - d, 16)]
            rcopy(
                block, block, sem_s[f"ret_{h}"].at[d], sem_r[f"ret_{h}"].at[d], (x, y, mod(e + 1, 16))
            ).wait_recv()

    weights = S.wt[...]
    for h in range(2):
        half = slice(h * (D // 2), (h + 1) * (D // 2))
        mixed = S.hid[:, half]
        for i in range(16):
            pair_rows = getattr(S, f"back_{h}")[i].astype(F32)
            for m in range(2):
                j = 2 * i + m
                mixed = mixed + weights[:, j : j + 1] * pair_rows[m : m + 1, :]
        out_ref[:, half] = mixed.astype(BF16)

    for copy in drains:
        copy.wait_send()
    for ring in (win0, win1, mix, gat, ow1, ow2, *ag1, *ag2[0], *ag2[1], *red1, *red2):
        ring.drain()
    for d in range(1, 16):

        @pl.when(s + d < 16)
        def _():
            sum_copy(d).wait_send()
            state_copy(d).wait_send()


def local_step(
    tokens, norm_gain, in_weight, conv_weight, conv_bias, proj_weight, step_weight, step_bias, decay_log,
    skip_gain, out_weight, moe_gain, router_weight, routes, gate_weight, up_weight, down_weight,
):
    operands = (
        tokens, norm_gain[None], in_weight, conv_weight, conv_bias[None],
        jnp.transpose(proj_weight), step_weight, step_bias[None], jnp.transpose(decay_log), skip_gain[None],
        out_weight.reshape(2, C // 2, FD), moe_gain[None], jnp.transpose(router_weight), jnp.transpose(routes),
        jnp.transpose(gate_weight[0]), jnp.transpose(up_weight[0]), down_weight[0],
    )
    spaces = {"v": pltpu.VMEM, "a": pl.ANY}
    return pl.pallas_call(
        kernel,
        out_shape=jax.ShapeDtypeStruct((8, D), BF16),
        in_specs=[pl.BlockSpec(memory_space=spaces[kind]) for _, kind in INPUTS],
        out_specs=pl.BlockSpec(memory_space=pltpu.VMEM),
        scratch_shapes=[pltpu.VMEM(shape, dtype) for shape, dtype in SCRATCH.values()]
        + [pltpu.SemaphoreType.DMA((count,)) for count in SEMS.values()] * 2,
        compiler_params=pltpu.CompilerParams(
            collective_id=0, has_side_effects=True, vmem_limit_bytes=60 * 1024 * 1024
        ),
    )(*operands)


def solution(mesh):
    split = Mesh(mesh.devices.reshape(4, 4, mesh.shape["expert"]), ("seq_0", "seq_1", "expert"))
    in_specs = (
        P(SEQ, None),
        P(),
        P(SEQ, None, "expert"),
        P(None, "expert"),
        P("expert"),
        P("expert", None),
        P(None, "expert"),
        P("expert"),
        P("expert", None),
        P("expert"),
        P("expert", SEQ),
        P(),
        P(),
        P(SEQ_EXPERT, None),
        P("expert", None, SEQ),
        P("expert", None, SEQ),
        P("expert", SEQ, None),
    )
    out_specs = P(SEQ_EXPERT, None)
    return jax.shard_map(local_step, mesh=split, in_specs=in_specs, out_specs=out_specs, check_vma=False)
```
